32 devices in a mesh: pipe: 4 (over z), expert: 8 (over y, x, core).
Axes of the slice: x: 2, y: 2, z: 4, core: 2. Of those that a mesh axis runs over, the one named last changes fastest.
Arguments:
- acts: bfloat16 [4, 64, 3584], P('pipe', 'expert'), may hold values from -6 to 6
- grads: bfloat16 [4, 64, 3584], P('pipe', 'expert'), may hold values from -6 to 6
- norm_gain: float32 [4, 3584], P('pipe'), may hold values from 0.1 to 1.9
- router: float32 [4, 3584, 8], P('pipe'), may hold values from -0.09375 to 0.09375
- w_gate: bfloat16 [4, 3584, 8192], P('pipe', None, 'expert'), may hold values from -0.09375 to 0.09375
- w_up: bfloat16 [4, 3584, 8192], P('pipe', None, 'expert'), may hold values from -0.09375 to 0.09375
- w_down: bfloat16 [4, 8192, 3584], P('pipe', 'expert'), may hold values from -0.1875 to 0.1875
- expert_ids: int32 [4, 64, 2], P('pipe', 'expert'), may hold values from 0 to 7, all different within a row; in each aligned block of 8 rows (0 to 7, 8 to 15, ..., all dimensions but the last counted through in order) at most 4 rows name the same one
Outputs:
- arrived: bfloat16 [4, 64, 3584], P('pipe', 'expert')
- returned: bfloat16 [4, 64, 3584], P('pipe', 'expert')
The draws below stay inside these ranges and needn't reach their ends.
Inputs may be any that keep to these rules, and one draw needn't show every extreme that they name: `expert_ids`: A token's 2 experts differ. Within the tokens of one device (aligned blocks of 8 tokens of one section), no expert is chosen more than 4 times, and some block chooses some expert exactly 4 times.
All inputs are finite; a program needn't handle non-finite values.
Results may differ from the reference program's by a relative error of at most 0.0058.
Values may be sent and summed in bfloat16 or wider, within the bound.
No kernel may reach another device: no remote copies, remote signals or barrier semaphores. Data moves between devices by JAX's collectives and lax.ppermute only.
A program may use at most 64 MiB of HBM per device.

```python
import math
import jax
import jax.numpy as jnp
import numpy as np
from jax import lax

D = 3584
EXP_FF = 1024
EXPERTS = 8
TOP = 2
TOK_DEV = 8
CAP = 4
G = 1
FF_DEV = 1024
TOKENS = 64
N_PIPE = 4
N_EXPERT = 8


def levels(rng, shape, shards, least, largest):
    factor_of = 1.0
    for axis_at, blocks in shards:
        steps = jax.random.uniform(jax.random.fold_in(jax.random.fold_in(rng, 6), axis_at), (blocks,), jnp.float32, least / len(shards), largest / len(shards))
        factor_of = factor_of * jnp.repeat(jnp.exp(steps), shape[axis_at] // blocks).reshape((-1,) + (1,) * (len(shape) - 1 - axis_at))
    return factor_of


def routed_block(own_key, own, number, rows, count, top, limit, skew):
    sequence = jax.random.permutation(own_key, count)
    packed, ordinary = portions_of(count, rows * top, limit, skew, True), portions_of(count, rows * top, limit, skew, False)
    places = jnp.arange(count)

    def named(tallies, rotation):
        used = int((tallies > 0).sum())
        fixed = max(1, used // 4)
        passed = fixed + (places - fixed + rotation * (used - fixed)) % max(1, count - fixed)
        return jnp.zeros((count,), jnp.int32).at[sequence[jnp.where(places < fixed, places, passed)]].set(jnp.asarray(tallies, jnp.int32))

    tallies = jnp.where(number % 4 == 0, named(packed, number // 4), named(ordinary, number - number // 4 - 1))
    mixed = jax.random.permutation(jax.random.fold_in(own, 3), count)
    source_of, sink = mixed[0:count // 2 * 2:2], mixed[1:count // 2 * 2:2]
    room = jnp.minimum(tallies[source_of] - 1, limit - tallies[sink]) // 2
    room = jnp.where((source_of == sequence[0]) | (sink == sequence[0]) | (tallies[sink] == 0), 0, jnp.maximum(room, 0))
    passed = jax.random.randint(jax.random.fold_in(own, 4), (count // 2,), 0, 1 << 20) % (room + 1)
    tallies = tallies.at[source_of].add(-passed).at[sink].add(passed)
    labels = jnp.searchsorted(jnp.cumsum(tallies), jnp.arange(rows * top), side="right").astype(jnp.int32)
    listing = labels.reshape(top, rows).T
    listing = listing[jax.random.permutation(jax.random.fold_in(own, 1), rows)]
    rotation = jax.random.randint(jax.random.fold_in(own, 2), (rows, 1), 0, top)
    return jnp.take_along_axis(listing, (jnp.arange(top)[None, :] + rotation) % top, axis=1)


def portions_of(number_of, total, limit, lean, full):
    portions = [(1 << 20) // math.isqrt(grade ** lean) + 1 for grade in range(1, number_of + 1)]
    largest = limit if full else min(limit, max(-(-total // number_of), total * portions[0] // sum(portions)))
    least = 1 if total - largest >= number_of - 1 else 0
    given, spare = [largest] + [least] * (number_of - 1), total - largest - least * (number_of - 1)
    while spare > 0:
        candidates = [i for i in range(1, number_of) if given[i] < largest] or [i for i in range(1, number_of) if given[i] < limit]
        pool, remaining = sum([portions[i] for i in candidates]), spare
        for i in candidates:
            extra = min(limit - given[i], max(1, remaining * portions[i] // pool), spare)
            given[i] = given[i] + extra
            spare = spare - extra
    return np.array(given)


def normal_values(stream_key, dims, scale, most, split=(), kind=jnp.bfloat16):
    loudness = levels(stream_key, dims, split, -0.22, 0.18) if split else 1.0
    array = jax.random.normal(stream_key, dims, jnp.float32) * scale * loudness
    return jnp.minimum(jnp.maximum(array, -most), most).astype(kind)


def setup_inputs(seed: int = 0) -> dict:
    key_of = jax.random.split(jax.random.key(seed), 9)
    acts = normal_values(key_of[0], (N_PIPE, TOKENS, D), 1.0, 6.0, ((0, 4), (1, 8)))
    grads = normal_values(key_of[1], (N_PIPE, TOKENS, D), 1.0, 6.0, ((0, 4), (1, 8)))
    norm_gain = jnp.clip(1.0 + 0.18 * jax.random.normal(key_of[2], (N_PIPE, D), jnp.float32), 0.1, 1.9)
    router = normal_values(key_of[3], (N_PIPE, D, EXPERTS), D ** -0.5, 0.09375, ((0, 4),), jnp.float32)
    w_gate = normal_values(key_of[4], (N_PIPE, D, EXPERTS * EXP_FF), D ** -0.5, 0.09375, ((0, 4), (2, 8)))
    w_up = normal_values(key_of[5], (N_PIPE, D, EXPERTS * EXP_FF), D ** -0.5, 0.09375, ((0, 4), (2, 8)))
    w_down = normal_values(key_of[6], (N_PIPE, EXPERTS * EXP_FF, D), EXP_FF ** -0.5, 0.1875, ((0, 4), (1, 8)))
    expert_ids_keys = jax.random.split(jax.random.fold_in(key_of[7], 1), N_PIPE * TOKENS // TOK_DEV)
    expert_ids_turns = jax.random.permutation(jax.random.fold_in(key_of[7], 3), N_PIPE * TOKENS // TOK_DEV)
    expert_ids = jax.vmap(lambda own, number: routed_block(jax.random.fold_in(key_of[7], 2), own, number, TOK_DEV, EXPERTS, TOP, CAP, 2))(expert_ids_keys, expert_ids_turns).reshape((N_PIPE, TOKENS, TOP))
    return dict(acts=acts, grads=grads, norm_gain=norm_gain, router=router, w_gate=w_gate, w_up=w_up, w_down=w_down, expert_ids=expert_ids)


EPS = 1e-06

def silu_parts(gate):
    sigma = jax.nn.sigmoid(gate)
    return (gate * sigma, sigma * (1.0 + gate * (1.0 - sigma)))

def slot_tables(pair_ids):
    expert_range = jnp.arange(EXPERTS, dtype=jnp.int32)
    chosen = (pair_ids[:, :, None] == expert_range[None, None, :]).astype(jnp.int32)
    earlier = jnp.cumsum(chosen, axis=1) - chosen
    position = lax.optimization_barrier(jnp.sum(earlier * chosen, axis=2))
    slot_range = jnp.arange(CAP, dtype=jnp.int32)
    slot_hit = (position[:, None, :] == slot_range[None, :, None]).astype(jnp.int32)
    table = jnp.transpose(chosen, (0, 2, 1))[:, :, None, :] * slot_hit[:, None, :, :]
    return table.astype(jnp.float32)

def expert_rows(rows_x, rows_g, gate_w, up_w, down_w):
    count = rows_x.shape[0]
    gate = jnp.dot(rows_x, gate_w, preferred_element_type=jnp.float32)
    upper = jnp.dot(rows_x, up_w, preferred_element_type=jnp.float32)
    active, slope = silu_parts(gate)
    hidden = (active * upper).astype(jnp.bfloat16)
    down_split = down_w.reshape(G, FF_DEV, D).astype(jnp.float32)
    hidden_split = hidden.reshape(count, G, FF_DEV).astype(jnp.float32)
    part_out = jnp.einsum('rgf,gfd->rgd', hidden_split, down_split).astype(jnp.bfloat16)
    dhidden = lax.dot_general(rows_g, down_w, (((1,), (1,)), ((), ())), preferred_element_type=jnp.float32)
    dgate = (dhidden * upper * slope).astype(jnp.bfloat16)
    dupper = (dhidden * active).astype(jnp.bfloat16)
    gate_split = gate_w.reshape(D, G, FF_DEV).astype(jnp.float32)
    up_split = up_w.reshape(D, G, FF_DEV).astype(jnp.float32)
    first = jnp.einsum('rgf,dgf->rgd', dgate.reshape(count, G, FF_DEV).astype(jnp.float32), gate_split)
    second = jnp.einsum('rgf,dgf->rgd', dupper.reshape(count, G, FF_DEV).astype(jnp.float32), up_split)
    part_din = (first + second).astype(jnp.bfloat16)
    return (part_out, part_din)

def section(section_input, section_dy, gain, route_w, gate_all, up_all, down_all, choice_ids):
    xvals = section_input.astype(jnp.float32)
    inverse_rms = lax.rsqrt(lax.optimization_barrier(jnp.mean(xvals * xvals, axis=-1, keepdims=True)) + EPS)
    normed = (xvals * inverse_rms * gain).astype(jnp.bfloat16)
    logits = jnp.dot(normed.astype(jnp.float32), route_w, precision=lax.Precision.HIGHEST)
    affinity = jax.nn.sigmoid(logits)
    expert_range = jnp.arange(EXPERTS, dtype=jnp.int32)
    chosen = (choice_ids[:, :, None] == expert_range[None, None, :]).astype(jnp.float32)
    selected = lax.optimization_barrier(jnp.sum(chosen * affinity[:, None, :], axis=-1))
    total = lax.optimization_barrier(jnp.sum(selected, axis=-1, keepdims=True))
    weight = selected / total
    dyvals = section_dy.astype(jnp.float32)
    scaled_grad = (weight[:, :, None] * dyvals[:, None, :]).astype(jnp.bfloat16)
    pairs = TOK_DEV * TOP
    table = slot_tables(choice_ids.reshape(N_EXPERT, pairs))
    pair_x = jnp.broadcast_to(normed[:, None, :], (TOKENS, TOP, D)).reshape(N_EXPERT, pairs, D)
    pair_g = scaled_grad.reshape(N_EXPERT, pairs, D)
    sent_x = jnp.einsum('secp,spd->escd', table, pair_x.astype(jnp.float32)).astype(jnp.bfloat16)
    sent_g = jnp.einsum('secp,spd->escd', table, pair_g.astype(jnp.float32)).astype(jnp.bfloat16)
    sent_x = sent_x.reshape(EXPERTS, N_EXPERT * CAP, D)
    sent_g = sent_g.reshape(EXPERTS, N_EXPERT * CAP, D)
    gate_e = jnp.transpose(gate_all.reshape(D, EXPERTS, EXP_FF), (1, 0, 2))
    up_e = jnp.transpose(up_all.reshape(D, EXPERTS, EXP_FF), (1, 0, 2))
    down_e = down_all.reshape(EXPERTS, EXP_FF, D)

    def one_expert(items):
        return expert_rows(*items)
    part_out, part_din = lax.map(one_expert, (sent_x, sent_g, gate_e, up_e, down_e))
    part_out = part_out.reshape(EXPERTS, N_EXPERT, CAP, G, D).astype(jnp.float32)
    part_din = part_din.reshape(EXPERTS, N_EXPERT, CAP, G, D).astype(jnp.float32)
    expert_out = jnp.einsum('secp,escgd->spd', table, part_out).reshape(TOKENS, TOP, D)
    expert_din = jnp.einsum('secp,escgd->spd', table, part_din).reshape(TOKENS, TOP, D)
    section_out = (xvals + lax.optimization_barrier(jnp.sum(weight[:, :, None] * expert_out, axis=1))).astype(jnp.bfloat16)
    dweight = lax.optimization_barrier(jnp.sum(dyvals[:, None, :] * expert_out, axis=-1))
    mixed = lax.optimization_barrier(jnp.sum(weight * dweight, axis=-1, keepdims=True))
    dselect = (dweight - mixed) / total
    dlogit_pair = dselect * selected * (1.0 - selected)
    dlogit = lax.optimization_barrier(jnp.sum(chosen * dlogit_pair[:, :, None], axis=1))
    from_router = lax.dot_general(dlogit, route_w, (((1,), (1,)), ((), ())), precision=lax.Precision.HIGHEST)
    dnormed = lax.optimization_barrier(jnp.sum(expert_din, axis=1)) + from_router
    scaled_u = gain * dnormed
    dnorm = inverse_rms * scaled_u - xvals * inverse_rms ** 3 * lax.optimization_barrier(jnp.mean(scaled_u * xvals, axis=-1, keepdims=True))
    section_grad = (dyvals + dnorm).astype(jnp.bfloat16)
    return (section_out, section_grad)

def reference(acts, grads, norm_gain, router, w_gate, w_up, w_down, expert_ids):

    def one_section(items):
        return section(*items)
    outputs, input_grads = lax.map(one_section, (acts, grads, norm_gain, router, w_gate, w_up, w_down, expert_ids))
    zero_block = jnp.zeros_like(outputs[:1])
    arrived = jnp.concatenate([zero_block, outputs[:-1]], axis=0)
    returned = jnp.concatenate([input_grads[1:], zero_block], axis=0)
    return (arrived, returned)
```

```python
import functools
import jax
import jax.numpy as jnp
from jax import lax
from jax.experimental import pallas as pl
from jax.experimental.pallas import tpu as pltpu
from jax.sharding import PartitionSpec as P

EXPERTS = 8
LANES = 128
EPS = 1e-06
F32 = jnp.float32
BF16 = jnp.bfloat16


VMEM = pl.BlockSpec(memory_space=pltpu.VMEM)
SMEM = pl.BlockSpec(memory_space=pltpu.SMEM)


def flip(value, bit):
    count = lax.axis_size("expert")
    return lax.ppermute(value, "expert", [(i, i ^ bit) for i in range(count)])


def pack_kernel(x_ref, g_ref, ids_ref, o_ref):
    rows, width = x_ref.shape
    o_ref[0, :rows, :width] = x_ref[...]
    o_ref[0, rows:, :width] = g_ref[...]
    lane = lax.broadcasted_iota(jnp.int32, (rows, LANES), 1)
    ids = ids_ref[...]
    tail = jnp.zeros((rows, LANES), F32)
    for k in range(ids.shape[1]):
        tail = jnp.where(lane == k, ids[:, k : k + 1].astype(F32), tail)
    o_ref[0, :rows, width:] = tail.astype(BF16)
    o_ref[0, rows:, width:] = jnp.zeros((rows, LANES), BF16)


def pack(x, g, ids):
    rows, width = x.shape
    return pl.pallas_call(
        pack_kernel,
        out_shape=jax.ShapeDtypeStruct((1, 2 * rows, width + LANES), BF16),
        in_specs=[VMEM] * 3,
        out_specs=VMEM,
        name="pack",
        cost_estimate=pl.CostEstimate(flops=0, bytes_accessed=8 * rows * width, transcendentals=0),
    )(x, g, ids)


def contract_last(left, right):
    return lax.dot_general(left, right, (((1,), (1,)), ((), ())), preferred_element_type=F32)


def expert_kernel(top, me_ref, gain_ref, router_ref, wg_ref, wu_ref, wd_ref, *refs):
    pieces, outs = refs[:8], refs[8:16]
    nb, sg, gate_s, up_s, out_s, hid_s, dg_s, du_s = refs[16:]
    blocks, double, wide = pieces[0].shape
    rows = double // 2
    width, units = wg_ref.shape
    step_f = min(units, 256)
    step_d = 512 if width % 512 == 0 else width
    mine = me_ref[0]
    gain = gain_ref[...]
    router = router_ref[...]
    r_hi = router.astype(BF16)
    rest = router - r_hi.astype(F32)
    r_mid = rest.astype(BF16)
    r_lo = (rest - r_mid.astype(F32)).astype(BF16)
    split = jnp.concatenate([r_hi, r_mid, r_lo], axis=0)
    total_rows = 8 * rows
    lane = lax.broadcasted_iota(jnp.int32, (total_rows, EXPERTS), 1)

    def block(h, carry):
        x = jnp.concatenate([p[h, :rows, :width].astype(F32) for p in pieces], axis=0)
        dy = jnp.concatenate([p[h, rows:, :width].astype(F32) for p in pieces], axis=0)
        ids = jnp.concatenate([p[h, :rows, width:].astype(F32) for p in pieces], axis=0)
        inv = lax.rsqrt(jnp.mean(x * x, axis=-1, keepdims=True) + EPS)
        nb[...] = (x * inv * gain).astype(BF16)
        parts = contract_last(nb[...], split)
        logits = parts[:, :EXPERTS] + parts[:, EXPERTS : 2 * EXPERTS] + parts[:, 2 * EXPERTS :]
        affinity = 1.0 / (1.0 + jnp.exp(-logits))
        chosen = jnp.zeros((total_rows, EXPERTS), F32)
        for k in range(top):
            chosen += (ids[:, k : k + 1].astype(jnp.int32) == lane).astype(F32)
        total = jnp.sum(chosen * affinity, axis=-1, keepdims=True)
        here = chosen * (lane == mine).astype(F32)
        has = jnp.sum(here, axis=-1, keepdims=True)
        weight = jnp.sum(here * affinity, axis=-1, keepdims=True) / total
        sg[...] = (weight * dy).astype(BF16)

        def first(n, c):
            cols = pl.ds(pl.multiple_of(n * step_f, step_f), step_f)
            gate_s[:, cols] = jnp.dot(nb[...], wg_ref[:, cols], preferred_element_type=F32)
            up_s[:, cols] = jnp.dot(nb[...], wu_ref[:, cols], preferred_element_type=F32)
            return c

        lax.fori_loop(0, units // step_f, first, 0)
        gate = gate_s[...]
        up = up_s[...]
        sigma = 1.0 / (1.0 + jnp.exp(-gate))
        active = gate * sigma
        slope = sigma * (1.0 + gate * (1.0 - sigma))
        hid_s[...] = (active * up).astype(BF16)

        def second(n, c):
            cols = pl.ds(pl.multiple_of(n * step_d, step_d), step_d)
            out_s[:, cols] = jnp.dot(hid_s[...], wd_ref[:, cols], preferred_element_type=F32)
            return c

        lax.fori_loop(0, width // step_d, second, 0)
        out = out_s[...]
        dweight = has * jnp.sum(dy * out, axis=-1, keepdims=True)
        share = (weight * out).astype(BF16)
        for q in range(8):
            outs[q][h, :rows, :] = share[q * rows : (q + 1) * rows]
        coef = chosen * affinity * (1.0 - affinity) * ((lane == mine).astype(F32) - weight)
        coef = coef * (dweight / total)

        def third(n, c):
            cols = pl.ds(pl.multiple_of(n * step_f, step_f), step_f)
            gate_s[:, cols] = contract_last(sg[...], wd_ref[cols, :])
            return c

        lax.fori_loop(0, units // step_f, third, 0)
        dhidden = gate_s[...]
        dg_s[...] = (dhidden * up * slope).astype(BF16)
        du_s[...] = (dhidden * active).astype(BF16)

        def fourth(n, c):
            cols = pl.ds(pl.multiple_of(n * step_d, step_d), step_d)
            out_s[:, cols] = (
                contract_last(dg_s[...], wg_ref[cols, :])
                + contract_last(du_s[...], wu_ref[cols, :])
                + jnp.dot(coef, router_ref[:, cols], precision=lax.Precision.HIGHEST, preferred_element_type=F32)
            )
            return c

        lax.fori_loop(0, width // step_d, fourth, 0)
        u = out_s[...] * gain
        x = jnp.concatenate([p[h, :rows, :width].astype(F32) for p in pieces], axis=0)
        m = jnp.mean(u * x, axis=-1, keepdims=True)
        din = (inv * u - x * (inv * inv * inv * m)).astype(BF16)
        for q in range(8):
            outs[q][h, rows:, :] = din[q * rows : (q + 1) * rows]
        return carry

    lax.fori_loop(0, blocks, block, 0)


def experts(top, me, gain, router, wg, wu, wd, pieces):
    blocks, double, wide = pieces[0].shape
    width, units = wg.shape
    total = 8 * double // 2
    return pl.pallas_call(
        functools.partial(expert_kernel, top),
        out_shape=[jax.ShapeDtypeStruct((blocks, double, width), BF16)] * 8,
        in_specs=[SMEM] + [VMEM] * (5 + 8),
        out_specs=[VMEM] * 8,
        scratch_shapes=[
            pltpu.VMEM((total, width), BF16),
            pltpu.VMEM((total, width), BF16),
            pltpu.VMEM((total, units), F32),
            pltpu.VMEM((total, units), F32),
            pltpu.VMEM((total, width), F32),
            pltpu.VMEM((total, units), BF16),
            pltpu.VMEM((total, units), BF16),
            pltpu.VMEM((total, units), BF16),
        ],
        compiler_params=pltpu.CompilerParams(vmem_limit_bytes=VMEM_LIMIT),
        name="experts",
    )(me, gain, router, wg, wu, wd, *pieces)


VMEM_LIMIT = 24 << 20


def add(a, b):
    return (a.astype(F32) + b.astype(F32)).astype(BF16)


def on_device(acts, grads, norm_gain, router, w_gate, w_up, w_down, expert_ids):
    x, dy, ids = acts[0], grads[0], expert_ids[0]
    rows, width = x.shape
    count = lax.axis_size("expert")
    groups = count // EXPERTS
    own = pack(x, dy, ids)
    bit = 8
    while bit < count:
        own = jnp.concatenate([own, flip(own, bit)], axis=0)
        bit *= 2
    pieces = {0: own}
    for j in (6, 2, 4):
        pieces[j] = flip(own, j)
    for j in (0, 2, 4, 6):
        pieces[j + 1] = flip(pieces[j], 1)
    me = (lax.axis_index("expert") // groups).astype(jnp.int32).reshape(1)
    outs = experts(
        ids.shape[1], me, norm_gain, router[0].T, w_gate[0], w_up[0], w_down[0],
        [pieces[j] for j in range(8)],
    )
    kept = {j: add(outs[j], flip(outs[j + 1], 1)) for j in (6, 2, 4, 0)}
    came = [flip(kept[j], j) for j in (6, 2, 4)]
    if count > 8:
        got = kept[0].astype(F32) + sum(c.astype(F32) for c in came)
        bit = count // 2
        while bit >= 8:
            half = got.shape[0] // 2
            got = got[:half] + flip(got[half:].astype(BF16), bit).astype(F32)
            bit //= 2
    else:
        got = kept[0].astype(F32) + sum(c.astype(F32) for c in came)
    section_out = (x.astype(F32) + got[0, :rows]).astype(BF16)
    section_grad = (dy.astype(F32) + got[0, rows:]).astype(BF16)
    stages = lax.axis_size("pipe")
    odd = lax.axis_index("pipe") % 2 == 1
    first = jnp.where(odd, section_grad, section_out)
    second = jnp.where(odd, section_out, section_grad)

    def trade(value, parity):
        pairs = []
        for s in range(parity, stages - 1, 2):
            pairs += [(s, s + 1), (s + 1, s)]
        return lax.ppermute(value, "pipe", pairs)

    second = trade(second, 1)
    first = trade(first, 0)
    arrived = jnp.where(odd, first, second)
    returned = jnp.where(odd, second, first)
    return (arrived[None], returned[None])


def solution(mesh):
    return jax.shard_map(
        on_device,
        mesh=mesh,
        in_specs=(
            P("pipe", "expert", None),
            P("pipe", "expert", None),
            P("pipe", None),
            P("pipe", None, None),
            P("pipe", None, "expert"),
            P("pipe", None, "expert"),
            P("pipe", "expert", None),
            P("pipe", "expert", None),
        ),
        out_specs=(P("pipe", "expert", None), P("pipe", "expert", None)),
        check_vma=False,
    )
```

```python
import functools
import jax
import jax.numpy as jnp
from jax import lax
from jax.experimental import pallas as pl
from jax.experimental.pallas import tpu as pltpu
from jax.sharding import PartitionSpec as P

EXPERTS = 8
LANES = 128
EPS = 1e-06
F32 = jnp.float32
BF16 = jnp.bfloat16


VMEM = pl.BlockSpec(memory_space=pltpu.VMEM)
HBM = pl.BlockSpec(memory_space=pltpu.HBM)
SMEM = pl.BlockSpec(memory_space=pltpu.SMEM)


def flip(value, bit):
    count = lax.axis_size("expert")
    return lax.ppermute(value, "expert", [(i, i ^ bit) for i in range(count)])


def pack_kernel(x_hbm, g_hbm, ids_hbm, o_ref, ids_ref, sems):
    rows, width = x_hbm.shape
    copies = [
        pltpu.make_async_copy(ids_hbm, ids_ref, sems.at[0]),
        pltpu.make_async_copy(x_hbm, o_ref.at[0, pl.ds(0, rows), pl.ds(0, width)], sems.at[1]),
        pltpu.make_async_copy(g_hbm, o_ref.at[0, pl.ds(rows, rows), pl.ds(0, width)], sems.at[2]),
    ]
    for copy in copies:
        copy.start()
    o_ref[0, rows:, width:] = jnp.zeros((rows, LANES), BF16)
    lane = lax.broadcasted_iota(jnp.int32, (rows, LANES), 1)
    across = lax.broadcasted_iota(jnp.int32, (rows, rows), 1)
    down = lax.broadcasted_iota(jnp.int32, (rows, rows), 0)
    copies[0].wait()
    ids = ids_ref[...].astype(F32)
    tail = jnp.zeros((rows, LANES), F32)
    for k in range(ids.shape[0]):
        column = jnp.sum(jnp.where(across == down, ids[k : k + 1, :], 0.0), axis=1, keepdims=True)
        tail = jnp.where(lane == k, column, tail)
    o_ref[0, :rows, width:] = tail.astype(BF16)
    copies[1].wait()
    copies[2].wait()


def pack(x, g, ids):
    rows, width = x.shape
    return pl.pallas_call(
        pack_kernel,
        out_shape=jax.ShapeDtypeStruct((1, 2 * rows, width + LANES), BF16),
        in_specs=[HBM] * 3,
        out_specs=VMEM,
        scratch_shapes=[pltpu.VMEM(ids.shape, jnp.int32), pltpu.SemaphoreType.DMA((3,))],
        name="pack",
        cost_estimate=pl.CostEstimate(flops=0, bytes_accessed=8 * rows * width, transcendentals=0),
    )(x, g, ids)


def fetch_kernel(*refs):
    count = (len(refs) - 1) // 2
    sources, targets, sems = refs[:count], refs[count:-1], refs[-1]
    copies = [pltpu.make_async_copy(a, b, sems.at[i]) for i, (a, b) in enumerate(zip(sources, targets))]
    for copy in copies:
        copy.start()
    for copy in copies:
        copy.wait()


def fetch(*arrays):
    count = len(arrays)
    held = sum(a.size * a.dtype.itemsize for a in arrays)
    return pl.pallas_call(
        fetch_kernel,
        out_shape=[pltpu.VMEM(a.shape, a.dtype) for a in arrays],
        in_specs=[HBM] * count,
        out_specs=[VMEM] * count,
        scratch_shapes=[pltpu.SemaphoreType.DMA((count,))],
        name="fetch",
        compiler_params=pltpu.CompilerParams(vmem_limit_bytes=1 << 20),
        cost_estimate=pl.CostEstimate(flops=0, bytes_accessed=held, transcendentals=0),
    )(*[pltpu.with_memory_space_constraint(a, pltpu.HBM) for a in arrays])


def contract_last(left, right):
    return lax.dot_general(left, right, (((1,), (1,)), ((), ())), preferred_element_type=F32)


def expert_kernel(top, me_ref, gain_ref, router_ref, wg_ref, wu_ref, wd_hbm, *refs):
    pieces, outs = refs[:8], refs[8:16]
    nb, sg, gate_s, up_s, out_s, hid_s, dg_s, du_s, wd_ref, wd_sem = refs[16:]
    wd_copy = pltpu.make_async_copy(wd_hbm, wd_ref, wd_sem)
    wd_copy.start()
    blocks, double, wide = pieces[0].shape
    rows = double // 2
    width, units = wg_ref.shape
    step_f = units
    step_d = width // 2 if width % 256 == 0 else width
    mine = me_ref[0]
    gain = gain_ref[...]
    router = router_ref[...]
    r_hi = router.astype(BF16)
    rest = router - r_hi.astype(F32)
    r_mid = rest.astype(BF16)
    r_lo = (rest - r_mid.astype(F32)).astype(BF16)
    split = jnp.concatenate([r_hi, r_mid, r_lo], axis=0)
    total_rows = 8 * rows
    lane = lax.broadcasted_iota(jnp.int32, (total_rows, EXPERTS), 1)

    def block(h, carry):
        x = jnp.concatenate([p[h, :rows, :width].astype(F32) for p in pieces], axis=0)
        dy = jnp.concatenate([p[h, rows:, :width].astype(F32) for p in pieces], axis=0)
        ids = jnp.concatenate([p[h, :rows, width:].astype(F32) for p in pieces], axis=0)
        inv = lax.rsqrt(jnp.mean(x * x, axis=-1, keepdims=True) + EPS)
        nb[...] = (x * inv * gain).astype(BF16)
        parts = contract_last(nb[...], split)
        logits = parts[:, :EXPERTS] + parts[:, EXPERTS : 2 * EXPERTS] + parts[:, 2 * EXPERTS :]
        affinity = 1.0 / (1.0 + jnp.exp(-logits))
        chosen = jnp.zeros((total_rows, EXPERTS), F32)
        for k in range(top):
            chosen += (ids[:, k : k + 1].astype(jnp.int32) == lane).astype(F32)
        total = jnp.sum(chosen * affinity, axis=-1, keepdims=True)
        here = chosen * (lane == mine).astype(F32)
        has = jnp.sum(here, axis=-1, keepdims=True)
        weight = jnp.sum(here * affinity, axis=-1, keepdims=True) / total
        sg[...] = (weight * dy).astype(BF16)

        def first(n, c):
            cols = pl.ds(pl.multiple_of(n * step_f, step_f), step_f)
            gate_s[:, cols] = jnp.dot(nb[...], wg_ref[:, cols], preferred_element_type=F32)
            up_s[:, cols] = jnp.dot(nb[...], wu_ref[:, cols], preferred_element_type=F32)
            return c

        lax.fori_loop(0, units // step_f, first, 0)
        gate = gate_s[...]
        up = up_s[...]
        sigma = 1.0 / (1.0 + jnp.exp(-gate))
        active = gate * sigma
        slope = sigma * (1.0 + gate * (1.0 - sigma))
        hid_s[...] = (active * up).astype(BF16)

        if blocks == 1:
            wd_copy.wait()

        def second(n, c):
            cols = pl.ds(pl.multiple_of(n * step_d, step_d), step_d)
            out_s[:, cols] = jnp.dot(hid_s[...], wd_ref[:, cols], preferred_element_type=F32)
            return c

        lax.fori_loop(0, width // step_d, second, 0)
        out = out_s[...]
        dweight = has * jnp.sum(dy * out, axis=-1, keepdims=True)
        share = (weight * out).astype(BF16)
        for q in range(8):
            outs[q][h, :rows, :] = share[q * rows : (q + 1) * rows]
        coef = chosen * affinity * (1.0 - affinity) * ((lane == mine).astype(F32) - weight)
        coef = coef * (dweight / total)

        def third(n, c):
            cols = pl.ds(pl.multiple_of(n * step_f, step_f), step_f)
            gate_s[:, cols] = contract_last(sg[...], wd_ref[cols, :])
            return c

        lax.fori_loop(0, units // step_f, third, 0)
        dhidden = gate_s[...]
        dg_s[...] = (dhidden * up * slope).astype(BF16)
        du_s[...] = (dhidden * active).astype(BF16)

        def fourth(n, c):
            cols = pl.ds(pl.multiple_of(n * step_d, step_d), step_d)
            out_s[:, cols] = (
                contract_last(dg_s[...], wg_ref[cols, :])
                + contract_last(du_s[...], wu_ref[cols, :])
                + jnp.dot(coef, router_ref[:, cols], precision=lax.Precision.HIGHEST, preferred_element_type=F32)
            )
            return c

        lax.fori_loop(0, width // step_d, fourth, 0)
        u = out_s[...] * gain
        x = jnp.concatenate([p[h, :rows, :width].astype(F32) for p in pieces], axis=0)
        m = jnp.mean(u * x, axis=-1, keepdims=True)
        din = (inv * u - x * (inv * inv * inv * m)).astype(BF16)
        for q in range(8):
            outs[q][h, rows:, :] = din[q * rows : (q + 1) * rows]
        return carry

    if blocks == 1:
        block(0, 0)
    else:
        wd_copy.wait()
        lax.fori_loop(0, blocks, block, 0)


def experts(top, me, gain, router, wg, wu, wd, pieces):
    blocks, double, wide = pieces[0].shape
    width, units = wg.shape
    total = 8 * double // 2
    return pl.pallas_call(
        functools.partial(expert_kernel, top),
        out_shape=[jax.ShapeDtypeStruct((blocks, double, width), BF16)] * 8,
        in_specs=[SMEM] + [VMEM] * 4 + [HBM] + [VMEM] * 8,
        out_specs=[VMEM] * 8,
        scratch_shapes=[
            pltpu.VMEM((total, width), BF16),
            pltpu.VMEM((total, width), BF16),
            pltpu.VMEM((total, units), F32),
            pltpu.VMEM((total, units), F32),
            pltpu.VMEM((total, width), F32),
            pltpu.VMEM((total, units), BF16),
            pltpu.VMEM((total, units), BF16),
            pltpu.VMEM((total, units), BF16),
            pltpu.VMEM((units, width), BF16),
            pltpu.SemaphoreType.DMA,
        ],
        compiler_params=pltpu.CompilerParams(vmem_limit_bytes=VMEM_LIMIT),
        name="experts",
    )(me, gain, router, wg, wu, wd, *pieces)


VMEM_LIMIT = 24 << 20
VMEM_ALL = 67043328
FETCH_ROOM = 1 << 20


def add(a, b):
    return (a.astype(F32) + b.astype(F32)).astype(BF16)


def on_device(acts, grads, norm_gain, router, w_gate, w_up, w_down, expert_ids):
    x, dy, ids = acts[0], grads[0], expert_ids[0]
    rows, width = x.shape
    count = lax.axis_size("expert")
    groups = count // EXPERTS
    own = pack(x, dy, ids.T)
    bit = 8
    while bit < count:
        own = jnp.concatenate([own, flip(own, bit)], axis=0)
        bit *= 2
    wg, wu, route, gain, held = fetch(w_gate[0], w_up[0], router[0].T, norm_gain, own)
    pieces = {0: own}
    for j in (6, 2, 4):
        pieces[j] = flip(own, j)
    for j in (0, 2, 4, 6):
        pieces[j + 1] = flip(pieces[j], 1)
    me = (lax.axis_index("expert") // groups).astype(jnp.int32).reshape(1)
    outs = experts(
        ids.shape[1], me, gain, route, wg, wu, pltpu.with_memory_space_constraint(w_down[0], pltpu.HBM),
        [held] + [pieces[j] for j in range(1, 8)],
    )
    kept = {j: add(outs[j], flip(outs[j + 1], 1)) for j in (6, 2, 4, 0)}
    came = [flip(kept[j], j) for j in (6, 2, 4)]
    if count > 8:
        got = kept[0].astype(F32) + sum(c.astype(F32) for c in came)
        bit = count // 2
        while bit >= 8:
            half = got.shape[0] // 2
            got = got[:half] + flip(got[half:].astype(BF16), bit).astype(F32)
            bit //= 2
    else:
        got = kept[0].astype(F32) + sum(c.astype(F32) for c in came)
    section_out = (x.astype(F32) + got[0, :rows]).astype(BF16)
    section_grad = (dy.astype(F32) + got[0, rows:]).astype(BF16)
    stages = lax.axis_size("pipe")
    odd = lax.axis_index("pipe") % 2 == 1
    first = jnp.where(odd, section_grad, section_out)
    second = jnp.where(odd, section_out, section_grad)

    def trade(value, parity):
        pairs = []
        for s in range(parity, stages - 1, 2):
            pairs += [(s, s + 1), (s + 1, s)]
        return lax.ppermute(value, "pipe", pairs)

    second = trade(second, 1)
    first = trade(first, 0)
    arrived = jnp.where(odd, first, second)
    returned = jnp.where(odd, second, first)
    return (arrived[None], returned[None])


def solution(mesh):
    return jax.shard_map(
        on_device,
        mesh=mesh,
        in_specs=(
            P("pipe", "expert", None),
            P("pipe", "expert", None),
            P("pipe", None),
            P("pipe", None, None),
            P("pipe", None, "expert"),
            P("pipe", None, "expert"),
            P("pipe", "expert", None),
            P("pipe", "expert", None),
        ),
        out_specs=(P("pipe", "expert", None), P("pipe", "expert", None)),
        check_vma=False,
    )
```

```python
import functools
import jax
import jax.numpy as jnp
from jax import lax
from jax.experimental import pallas as pl
from jax.experimental.pallas import tpu as pltpu
from jax.sharding import PartitionSpec as P

EXPERTS = 8
LANES = 128
EPS = 1e-06
F32 = jnp.float32
BF16 = jnp.bfloat16


VMEM = pl.BlockSpec(memory_space=pltpu.VMEM)
HBM = pl.BlockSpec(memory_space=pltpu.HBM)
SMEM = pl.BlockSpec(memory_space=pltpu.SMEM)


def flip(value, bit):
    count = lax.axis_size("expert")
    return lax.ppermute(value, "expert", [(i, i ^ bit) for i in range(count)])


def pack_kernel(x_hbm, g_hbm, ids_hbm, o_ref, ids_ref, sems):
    rows, width = x_hbm.shape
    copies = [
        pltpu.make_async_copy(ids_hbm, ids_ref, sems.at[0]),
        pltpu.make_async_copy(x_hbm, o_ref.at[0, pl.ds(0, rows), pl.ds(0, width)], sems.at[1]),
        pltpu.make_async_copy(g_hbm, o_ref.at[0, pl.ds(rows, rows), pl.ds(0, width)], sems.at[2]),
    ]
    for copy in copies:
        copy.start()
    o_ref[0, rows:, width:] = jnp.zeros((rows, LANES), BF16)
    lane = lax.broadcasted_iota(jnp.int32, (rows, LANES), 1)
    across = lax.broadcasted_iota(jnp.int32, (rows, rows), 1)
    down = lax.broadcasted_iota(jnp.int32, (rows, rows), 0)
    copies[0].wait()
    ids = ids_ref[...].astype(F32)
    tail = jnp.zeros((rows, LANES), F32)
    for k in range(ids.shape[0]):
        column = jnp.sum(jnp.where(across == down, ids[k : k + 1, :], 0.0), axis=1, keepdims=True)
        tail = jnp.where(lane == k, column, tail)
    o_ref[0, :rows, width:] = tail.astype(BF16)
    copies[1].wait()
    copies[2].wait()


def pack(x, g, ids):
    rows, width = x.shape
    return pl.pallas_call(
        pack_kernel,
        out_shape=pltpu.VMEM((1, 2 * rows, width + LANES), BF16),
        in_specs=[HBM] * 3,
        out_specs=VMEM,
        scratch_shapes=[pltpu.VMEM(ids.shape, jnp.int32), pltpu.SemaphoreType.DMA((3,))],
        name="pack",
        compiler_params=pltpu.CompilerParams(vmem_limit_bytes=1 << 20),
        cost_estimate=pl.CostEstimate(flops=0, bytes_accessed=8 * rows * width, transcendentals=0),
    )(*[pltpu.with_memory_space_constraint(a, pltpu.HBM) for a in (x, g, ids)])


def fetch_kernel(*refs):
    count = (len(refs) - 3) // 2
    sources, targets, sems = refs[:count], refs[count + 2 : -1], refs[-1]
    copies = [pltpu.make_async_copy(a, b, sems.at[i]) for i, (a, b) in enumerate(zip(sources, targets))]
    for copy in copies:
        copy.start()
    for copy in copies:
        copy.wait()


def fetch(after, me, *arrays):
    count = len(arrays)
    held = sum(a.size * a.dtype.itemsize for a in arrays)
    return pl.pallas_call(
        fetch_kernel,
        out_shape=[pltpu.VMEM(a.shape, a.dtype) for a in arrays],
        in_specs=[HBM] * count + [pl.BlockSpec(memory_space=pl.ANY), SMEM],
        out_specs=[VMEM] * count,
        scratch_shapes=[pltpu.SemaphoreType.DMA((count,))],
        name="fetch",
        compiler_params=pltpu.CompilerParams(vmem_limit_bytes=1 << 20),
        cost_estimate=pl.CostEstimate(flops=0, bytes_accessed=held, transcendentals=0),
    )(*[pltpu.with_memory_space_constraint(a, pltpu.HBM) for a in arrays], after, me)


def contract_last(left, right):
    return lax.dot_general(left, right, (((1,), (1,)), ((), ())), preferred_element_type=F32)


def thirds(value):
    high = value.astype(BF16)
    rest = value - high.astype(F32)
    middle = rest.astype(BF16)
    return high, middle, (rest - middle.astype(F32)).astype(BF16)


def expert_kernel(top, me_ref, gain_ref, router_ref, wg_ref, wu_ref, wd_hbm, *refs):
    pieces, outs, base_ref = refs[:8], refs[8:12], refs[12]
    nb, db, din_s, hid_s, dg_s, du_s, route_s, wd_ref, wd_sem = refs[13:]
    wd_copy = pltpu.make_async_copy(wd_hbm, wd_ref, wd_sem)
    wd_copy.start()
    blocks, double, _ = pieces[0].shape
    rows = double // 2
    width, _ = wg_ref.shape
    mine = me_ref[0]
    odd = me_ref[1]
    gain = gain_ref[...]
    r_hi, r_mid, r_lo = thirds(router_ref[...])
    split = jnp.concatenate([r_hi, r_mid, r_lo], axis=0)
    route_s[...] = jnp.concatenate([r_hi, r_mid, r_lo, r_hi, r_mid, r_hi], axis=0)
    total_rows = 8 * rows
    lane = lax.broadcasted_iota(jnp.int32, (total_rows, EXPERTS), 1)

    def gathered(h, first, start, size):
        return jnp.concatenate(
            [p[h, first : first + rows, start : start + size].astype(F32) for p in pieces], axis=0
        )

    def block(h, carry):
        x = gathered(h, 0, 0, width)
        ids = gathered(h, 0, width, LANES)
        inv = lax.rsqrt(jnp.mean(x * x, axis=-1, keepdims=True) + EPS)
        nb[...] = (x * inv * gain).astype(BF16)
        gate = jnp.dot(nb[...], wg_ref[...], preferred_element_type=F32)
        up = jnp.dot(nb[...], wu_ref[...], preferred_element_type=F32)
        db[...] = gathered(h, rows, 0, width).astype(BF16)
        parts = contract_last(nb[...], split)
        logits = parts[:, :EXPERTS] + parts[:, EXPERTS : 2 * EXPERTS] + parts[:, 2 * EXPERTS :]
        affinity = 1.0 / (1.0 + jnp.exp(-logits))
        chosen = jnp.zeros((total_rows, EXPERTS), F32)
        for k in range(top):
            chosen += (ids[:, k : k + 1].astype(jnp.int32) == lane).astype(F32)
        total = jnp.sum(chosen * affinity, axis=-1, keepdims=True)
        here = chosen * (lane == mine).astype(F32)
        has = jnp.sum(here, axis=-1, keepdims=True)
        weight = jnp.sum(here * affinity, axis=-1, keepdims=True) / total
        sigma = 1.0 / (1.0 + jnp.exp(-gate))
        active = gate * sigma
        slope = sigma * (1.0 + gate * (1.0 - sigma))
        hidden = (active * up).astype(BF16)
        hid_s[...] = hidden
        if blocks == 1:
            wd_copy.wait()
        pulled = contract_last(db[...], wd_ref[...])
        dweight = has * jnp.sum(hidden.astype(F32) * pulled, axis=-1, keepdims=True)
        dhidden = weight * pulled
        dg_s[...] = (dhidden * up * slope).astype(BF16)
        du_s[...] = (dhidden * active).astype(BF16)
        coef = chosen * affinity * (1.0 - affinity) * ((lane == mine).astype(F32) - weight)
        c_hi, c_mid, c_lo = thirds(coef * (dweight / total))
        coefs = jnp.concatenate([c_hi, c_hi, c_hi, c_mid, c_mid, c_lo], axis=1)
        step = width // DIN_STEPS
        moment = jnp.zeros((total_rows, 1), F32)
        for n in range(DIN_STEPS):
            cols = slice(n * step, (n + 1) * step)
            u = gain_ref[:, cols] * (
                contract_last(dg_s[...], wg_ref[cols, :])
                + contract_last(du_s[...], wu_ref[cols, :])
                + jnp.dot(coefs, route_s[:, cols], preferred_element_type=F32)
            )
            din_s[:, cols] = u
            moment += jnp.sum(u * gathered(h, 0, n * step, step), axis=-1, keepdims=True)
        scale = inv * inv * inv * (moment / width)
        step = width // OUT_STEPS
        for n in range(OUT_STEPS):
            cols = slice(n * step, (n + 1) * step)
            out = jnp.dot(hid_s[...], wd_ref[:, cols], preferred_element_type=F32)
            share = (weight * out).astype(BF16)
            grad = (inv * din_s[:, cols] - gathered(h, 0, n * step, step) * scale).astype(BF16)
            for q in range(8):
                core = odd if q % 2 == 0 else 1 - odd
                outs[q // 2][h, odd, core, :, cols] = share[q * rows : (q + 1) * rows]
                outs[q // 2][h, 1 - odd, core, :, cols] = grad[q * rows : (q + 1) * rows]
        return carry

    for q in range(2):
        core = odd if q == 0 else 1 - odd
        base_ref[odd, core] = pieces[q][0, :rows, :width]
        base_ref[1 - odd, core] = pieces[q][0, rows:, :width]
    if blocks == 1:
        block(0, 0)
    else:
        wd_copy.wait()
        lax.fori_loop(0, blocks, block, 0)


def experts(top, me, gain, router, wg, wu, wd, pieces):
    blocks, double, _ = pieces[0].shape
    rows = double // 2
    width, units = wg.shape
    total = 8 * rows
    return pl.pallas_call(
        functools.partial(expert_kernel, top),
        out_shape=[jax.ShapeDtypeStruct((blocks, 2, 2, rows, width), BF16)] * 4
        + [jax.ShapeDtypeStruct((2, 2, rows, width), BF16)],
        in_specs=[SMEM] + [VMEM] * 4 + [HBM] + [VMEM] * 8,
        out_specs=[VMEM] * 5,
        scratch_shapes=[
            pltpu.VMEM((total, width), BF16),
            pltpu.VMEM((total, width), BF16),
            pltpu.VMEM((total, width), F32),
            pltpu.VMEM((total, units), BF16),
            pltpu.VMEM((total, units), BF16),
            pltpu.VMEM((total, units), BF16),
            pltpu.VMEM((6 * EXPERTS, width), BF16),
            pltpu.VMEM((units, width), BF16),
            pltpu.SemaphoreType.DMA,
        ],
        compiler_params=pltpu.CompilerParams(vmem_limit_bytes=VMEM_LIMIT),
        name="experts",
    )(me, gain, router, wg, wu, wd, *pieces)


DIN_STEPS = 1
OUT_STEPS = 2
VMEM_LIMIT = 24 << 20


def add(a, b):
    return (a.astype(F32) + b.astype(F32)).astype(BF16)


def section_step(acts, grads, norm_gain, router, w_gate, w_up, w_down, expert_ids):
    x, dy, ids = acts[0], grads[0], expert_ids[0]
    count = lax.axis_size("expert")
    groups = count // EXPERTS
    index = lax.axis_index("expert")
    parity = index % 2
    me = jnp.stack([index // groups, parity]).astype(jnp.int32)
    own = pack(x, dy, ids.T)
    bit = 8
    while bit < count:
        own = jnp.concatenate([own, flip(own, bit)], axis=0)
        bit *= 2
    wg, wu, route, gain = fetch(own, me, w_gate[0], w_up[0], router[0].T, norm_gain)
    pieces = {0: own}
    for j in (6, 2, 4):
        pieces[j] = flip(own, j)
    for j in (0, 2, 4, 6):
        pieces[j + 1] = flip(pieces[j], 1)
    outs = experts(
        ids.shape[1], me, gain, route, wg, wu, pltpu.with_memory_space_constraint(w_down[0], pltpu.HBM),
        [pieces[j] for j in range(8)],
    )
    parts, base = outs[:4], outs[4]
    kept = {c: add(parts[c // 2][:, 0], flip(parts[c // 2][:, 1], 1)) for c in (6, 2, 4, 0)}
    came = [flip(kept[c], c) for c in (6, 2, 4)]
    got = kept[0].astype(F32) + sum(c.astype(F32) for c in came)
    bit = count // 2
    while bit >= 8:
        half = got.shape[0] // 2
        got = got[:half] + flip(got[half:].astype(BF16), bit).astype(F32)
        bit //= 2
    result = (base[0].astype(F32) + got[0]).astype(BF16)
    stages = lax.axis_size("pipe")
    pairs = []
    for s in range(stages - 1):
        for i in range(0, count, 2):
            low, high = s * count + i, (s + 1) * count + i + 1
            pairs += [(low, high), (high, low)]
    result = lax.ppermute(result, ("pipe", "expert"), pairs)
    is_odd = parity == 1
    mine = jnp.where(is_odd, result[1], result[0])
    other = flip(jnp.where(is_odd, result[0], result[1]), 1)
    arrived = jnp.where(is_odd, mine, other)
    returned = jnp.where(is_odd, other, mine)
    return (arrived[None], returned[None])


def solution(mesh):
    return jax.shard_map(
        section_step,
        mesh=mesh,
        in_specs=(
            P("pipe", "expert", None),
            P("pipe", "expert", None),
            P("pipe", None),
            P("pipe", None, None),
            P("pipe", None, "expert"),
            P("pipe", None, "expert"),
            P("pipe", "expert", None),
            P("pipe", "expert", None),
        ),
        out_specs=(P("pipe", "expert", None), P("pipe", "expert", None)),
        check_vma=False,
    )
```

```python
import functools
import jax
import jax.numpy as jnp
from jax import lax
from jax.experimental import pallas as pl
from jax.experimental.pallas import tpu as pltpu
from jax.sharding import PartitionSpec as P

EXPERTS = 8
LANES = 128
EPS = 1e-06
F32 = jnp.float32
BF16 = jnp.bfloat16


VMEM = pl.BlockSpec(memory_space=pltpu.VMEM)
HBM = pl.BlockSpec(memory_space=pltpu.HBM)
SMEM = pl.BlockSpec(memory_space=pltpu.SMEM)


def flip(value, bit):
    count = lax.axis_size("expert")
    return lax.ppermute(value, "expert", [(i, i ^ bit) for i in range(count)])


def pack_kernel(x_hbm, g_hbm, ids_hbm, o_ref, ids_ref, sems):
    rows, width = x_hbm.shape
    copies = [
        pltpu.make_async_copy(ids_hbm, ids_ref, sems.at[0]),
        pltpu.make_async_copy(x_hbm, o_ref.at[0, pl.ds(0, rows), pl.ds(0, width)], sems.at[1]),
        pltpu.make_async_copy(g_hbm, o_ref.at[0, pl.ds(rows, rows), pl.ds(0, width)], sems.at[2]),
    ]
    for copy in copies:
        copy.start()
    o_ref[0, rows:, width:] = jnp.zeros((rows, LANES), BF16)
    lane = lax.broadcasted_iota(jnp.int32, (rows, LANES), 1)
    across = lax.broadcasted_iota(jnp.int32, (rows, rows), 1)
    down = lax.broadcasted_iota(jnp.int32, (rows, rows), 0)
    copies[0].wait()
    ids = ids_ref[...].astype(F32)
    tail = jnp.zeros((rows, LANES), F32)
    for k in range(ids.shape[0]):
        column = jnp.sum(jnp.where(across == down, ids[k : k + 1, :], 0.0), axis=1, keepdims=True)
        tail = jnp.where(lane == k, column, tail)
    o_ref[0, :rows, width:] = tail.astype(BF16)
    copies[1].wait()
    copies[2].wait()


def pack(x, g, ids):
    rows, width = x.shape
    return pl.pallas_call(
        pack_kernel,
        out_shape=pltpu.VMEM((1, 2 * rows, width + LANES), BF16),
        in_specs=[HBM] * 3,
        out_specs=VMEM,
        scratch_shapes=[pltpu.VMEM(ids.shape, jnp.int32), pltpu.SemaphoreType.DMA((3,))],
        name="pack",
        compiler_params=pltpu.CompilerParams(vmem_limit_bytes=1 << 20),
        cost_estimate=pl.CostEstimate(flops=0, bytes_accessed=8 * rows * width, transcendentals=0),
    )(*[pltpu.with_memory_space_constraint(a, pltpu.HBM) for a in (x, g, ids)])


def fetch_kernel(*refs):
    count = (len(refs) - 3) // 2
    sources, targets, sems = refs[:count], refs[count + 2 : -1], refs[-1]
    copies = [pltpu.make_async_copy(a, b, sems.at[i]) for i, (a, b) in enumerate(zip(sources, targets))]
    for copy in copies:
        copy.start()
    for copy in copies:
        copy.wait()


def fetch(after, me, *arrays):
    count = len(arrays)
    held = sum(a.size * a.dtype.itemsize for a in arrays)
    return pl.pallas_call(
        fetch_kernel,
        out_shape=[pltpu.VMEM(a.shape, a.dtype) for a in arrays],
        in_specs=[HBM] * count + [pl.BlockSpec(memory_space=pl.ANY), SMEM],
        out_specs=[VMEM] * count,
        scratch_shapes=[pltpu.SemaphoreType.DMA((count,))],
        name="fetch",
        compiler_params=pltpu.CompilerParams(vmem_limit_bytes=1 << 20),
        cost_estimate=pl.CostEstimate(flops=0, bytes_accessed=held, transcendentals=0),
    )(*[pltpu.with_memory_space_constraint(a, pltpu.HBM) for a in arrays], after, me)


def contract_last(left, right):
    return lax.dot_general(left, right, (((1,), (1,)), ((), ())), preferred_element_type=F32)


def thirds(value):
    high = value.astype(BF16)
    rest = value - high.astype(F32)
    middle = rest.astype(BF16)
    return high, middle, (rest - middle.astype(F32)).astype(BF16)


def expert_kernel(top, me_ref, gain_ref, router_ref, wg_ref, wu_ref, wd_hbm, *refs):
    pieces, outs = refs[:8], refs[8:16]
    nb, sg, gate_s, up_s, out_s, hid_s, dg_s, du_s, route_s, wd_ref, wd_sem = refs[16:]
    wd_copy = pltpu.make_async_copy(wd_hbm, wd_ref, wd_sem)
    wd_copy.start()
    blocks, double, _ = pieces[0].shape
    rows = double // 2
    width, units = wg_ref.shape
    step_f = units
    step_d = width
    mine = me_ref[0]
    gain = gain_ref[...]
    router = router_ref[...]
    r_hi, r_mid, r_lo = thirds(router)
    split = jnp.concatenate([r_hi, r_mid, r_lo], axis=0)
    route_s[...] = jnp.concatenate([r_hi, r_mid, r_lo, r_hi, r_mid, r_hi], axis=0)
    routes = route_s
    total_rows = 8 * rows
    lane = lax.broadcasted_iota(jnp.int32, (total_rows, EXPERTS), 1)

    def block(h, carry):
        x = jnp.concatenate([p[h, :rows, :width].astype(F32) for p in pieces], axis=0)
        dy = jnp.concatenate([p[h, rows:, :width].astype(F32) for p in pieces], axis=0)
        ids = jnp.concatenate([p[h, :rows, width:].astype(F32) for p in pieces], axis=0)
        inv = lax.rsqrt(jnp.mean(x * x, axis=-1, keepdims=True) + EPS)
        nb[...] = (x * inv * gain).astype(BF16)
        parts = contract_last(nb[...], split)
        logits = parts[:, :EXPERTS] + parts[:, EXPERTS : 2 * EXPERTS] + parts[:, 2 * EXPERTS :]
        affinity = 1.0 / (1.0 + jnp.exp(-logits))
        chosen = jnp.zeros((total_rows, EXPERTS), F32)
        for k in range(top):
            chosen += (ids[:, k : k + 1].astype(jnp.int32) == lane).astype(F32)
        total = jnp.sum(chosen * affinity, axis=-1, keepdims=True)
        here = chosen * (lane == mine).astype(F32)
        has = jnp.sum(here, axis=-1, keepdims=True)
        weight = jnp.sum(here * affinity, axis=-1, keepdims=True) / total
        sg[...] = (weight * dy).astype(BF16)

        def first(n, c):
            cols = pl.ds(n * step_f, step_f)
            gate_s[:, cols] = jnp.dot(nb[...], wg_ref[:, cols], preferred_element_type=F32)
            up_s[:, cols] = jnp.dot(nb[...], wu_ref[:, cols], preferred_element_type=F32)
            return c

        for n in range(units // step_f):
            first(n, 0)
        gate = gate_s[...]
        up = up_s[...]
        sigma = 1.0 / (1.0 + jnp.exp(-gate))
        active = gate * sigma
        slope = sigma * (1.0 + gate * (1.0 - sigma))
        hid_s[...] = (active * up).astype(BF16)

        if blocks == 1:
            wd_copy.wait()

        def second(n, c):
            cols = pl.ds(n * step_d, step_d)
            out_s[:, cols] = jnp.dot(hid_s[...], wd_ref[:, cols], preferred_element_type=F32)
            return c

        for n in range(width // step_d):
            second(n, 0)
        out = out_s[...]
        dweight = has * jnp.sum(dy * out, axis=-1, keepdims=True)
        share = (weight * out).astype(BF16)
        for q in range(8):
            outs[q][h, :rows, :] = share[q * rows : (q + 1) * rows]
        coef = chosen * affinity * (1.0 - affinity) * ((lane == mine).astype(F32) - weight)
        coef = coef * (dweight / total)
        c_hi, c_mid, c_lo = thirds(coef)
        coefs = jnp.concatenate([c_hi, c_hi, c_hi, c_mid, c_mid, c_lo], axis=1)

        def third(n, c):
            cols = pl.ds(n * step_f, step_f)
            gate_s[:, cols] = contract_last(sg[...], wd_ref[cols, :])
            return c

        for n in range(units // step_f):
            third(n, 0)
        dhidden = gate_s[...]
        dg_s[...] = (dhidden * up * slope).astype(BF16)
        du_s[...] = (dhidden * active).astype(BF16)

        def fourth(n, c):
            cols = pl.ds(n * step_d, step_d)
            out_s[:, cols] = (
                contract_last(dg_s[...], wg_ref[cols, :])
                + contract_last(du_s[...], wu_ref[cols, :])
                + jnp.dot(coefs, routes[:, cols], preferred_element_type=F32)
            )
            return c

        for n in range(width // step_d):
            fourth(n, 0)
        u = out_s[...] * gain
        x = jnp.concatenate([p[h, :rows, :width].astype(F32) for p in pieces], axis=0)
        m = jnp.mean(u * x, axis=-1, keepdims=True)
        din = (inv * u - x * (inv * inv * inv * m)).astype(BF16)
        for q in range(8):
            outs[q][h, rows:, :] = din[q * rows : (q + 1) * rows]
        return carry

    if blocks == 1:
        block(0, 0)
    else:
        wd_copy.wait()
        lax.fori_loop(0, blocks, block, 0)


def experts(top, me, gain, router, wg, wu, wd, pieces):
    blocks, double, _ = pieces[0].shape
    width, units = wg.shape
    total = 8 * double // 2
    return pl.pallas_call(
        functools.partial(expert_kernel, top),
        out_shape=[jax.ShapeDtypeStruct((blocks, double, width), BF16)] * 8,
        in_specs=[SMEM] + [VMEM] * 4 + [HBM] + [VMEM] * 8,
        out_specs=[VMEM] * 8,
        scratch_shapes=[
            pltpu.VMEM((total, width), BF16),
            pltpu.VMEM((total, width), BF16),
            pltpu.VMEM((total, units), F32),
            pltpu.VMEM((total, units), F32),
            pltpu.VMEM((total, width), F32),
            pltpu.VMEM((total, units), BF16),
            pltpu.VMEM((total, units), BF16),
            pltpu.VMEM((total, units), BF16),
            pltpu.VMEM((6 * EXPERTS, width), BF16),
            pltpu.VMEM((units, width), BF16),
            pltpu.SemaphoreType.DMA,
        ],
        compiler_params=pltpu.CompilerParams(vmem_limit_bytes=VMEM_LIMIT),
        name="experts",
    )(me, gain, router, wg, wu, wd, *pieces)


VMEM_LIMIT = 24 << 20


def add(a, b):
    return (a.astype(F32) + b.astype(F32)).astype(BF16)


def section_step(acts, grads, norm_gain, router, w_gate, w_up, w_down, expert_ids):
    x, dy, ids = acts[0], grads[0], expert_ids[0]
    rows, width = x.shape
    count = lax.axis_size("expert")
    groups = count // EXPERTS
    index = lax.axis_index("expert")
    stage = lax.axis_index("pipe")
    me = jnp.stack([index // groups, index, stage]).astype(jnp.int32)
    own = pack(x, dy, ids.T)
    bit = 8
    while bit < count:
        own = jnp.concatenate([own, flip(own, bit)], axis=0)
        bit *= 2
    wg, wu, route, gain = fetch(own, me, w_gate[0], w_up[0], router[0].T, norm_gain)
    pieces = {0: own}
    for j in (6, 2, 4):
        pieces[j] = flip(own, j)
    for j in (0, 2, 4, 6):
        pieces[j + 1] = flip(pieces[j], 1)
    outs = experts(
        ids.shape[1], me, gain, route, wg, wu, pltpu.with_memory_space_constraint(w_down[0], pltpu.HBM),
        [pieces[j] for j in range(8)],
    )
    outs, index, stage = lax.optimization_barrier((outs, index, stage))
    side = lax.rem(index, 2)
    role = lax.rem(index + stage, 2)

    def by_role(c, want, values):
        first = jnp.where(role == want, values[c][:, :rows, :width], values[c][:, rows:, :width])
        second = jnp.where(role == want, values[c + 1][:, :rows, :width], values[c + 1][:, rows:, :width])
        low = jnp.where(side == 0, first, second)
        high = jnp.where(side == 0, second, first)
        return jnp.stack([low, high], axis=1)

    kept = {c: add(by_role(c, 0, outs), flip(by_role(c, 1, outs), 1)) for c in (6, 2, 4, 0)}
    came = [flip(kept[c], c) for c in (6, 2, 4)]
    got = kept[0].astype(F32) + sum(c.astype(F32) for c in came)
    bit = count // 2
    while bit >= 8:
        half = got.shape[0] // 2
        got = got[:half] + flip(got[half:].astype(BF16), bit).astype(F32)
        bit //= 2
    base = by_role(0, 0, [pieces[0][:1], pieces[1][:1]])[0]
    result = (base.astype(F32) + got[0]).astype(BF16)
    stages = lax.axis_size("pipe")
    pairs = []
    for s in range(stages - 1):
        for i in range(s % 2, count, 2):
            low, high = s * count + i, (s + 1) * count + i
            pairs += [(low, high), (high, low)]
    result = lax.ppermute(result, ("pipe", "expert"), pairs)
    mine = jnp.where(side == 1, result[1], result[0])
    other = flip(jnp.where(side == 1, result[0], result[1]), 1)
    arrived = jnp.where(role == 1, mine, other)
    returned = jnp.where(role == 1, other, mine)
    return (arrived[None], returned[None])


def solution(mesh):
    return jax.shard_map(
        section_step,
        mesh=mesh,
        in_specs=(
            P("pipe", "expert", None),
            P("pipe", "expert", None),
            P("pipe", None),
            P("pipe", None, None),
            P("pipe", None, "expert"),
            P("pipe", None, "expert"),
            P("pipe", "expert", None),
            P("pipe", "expert", None),
        ),
        out_specs=(P("pipe", "expert", None), P("pipe", "expert", None)),
        check_vma=False,
    )
```

```python
import functools
import jax
import jax.numpy as jnp
from jax import lax
from jax.experimental import pallas as pl
from jax.experimental.pallas import tpu as pltpu
from jax.sharding import PartitionSpec as P

EXPERTS = 8
LANES = 128
EPS = 1e-06
F32 = jnp.float32
BF16 = jnp.bfloat16


VMEM = pl.BlockSpec(memory_space=pltpu.VMEM)
HBM = pl.BlockSpec(memory_space=pltpu.HBM)
SMEM = pl.BlockSpec(memory_space=pltpu.SMEM)


def flip(value, bit):
    count = lax.axis_size("expert")
    return lax.ppermute(value, "expert", [(i, i ^ bit) for i in range(count)])


def pack_kernel(x_hbm, g_hbm, ids_hbm, o_ref, ids_ref, sems):
    rows, width = x_hbm.shape
    copies = [
        pltpu.make_async_copy(ids_hbm, ids_ref, sems.at[0]),
        pltpu.make_async_copy(x_hbm, o_ref.at[0, pl.ds(0, rows), pl.ds(0, width)], sems.at[1]),
        pltpu.make_async_copy(g_hbm, o_ref.at[0, pl.ds(rows, rows), pl.ds(0, width)], sems.at[2]),
    ]
    for copy in copies:
        copy.start()
    o_ref[0, rows:, width:] = jnp.zeros((rows, LANES), BF16)
    lane = lax.broadcasted_iota(jnp.int32, (rows, LANES), 1)
    across = lax.broadcasted_iota(jnp.int32, (rows, rows), 1)
    down = lax.broadcasted_iota(jnp.int32, (rows, rows), 0)
    copies[0].wait()
    ids = ids_ref[...].astype(F32)
    tail = jnp.zeros((rows, LANES), F32)
    for k in range(ids.shape[0]):
        column = jnp.sum(jnp.where(across == down, ids[k : k + 1, :], 0.0), axis=1, keepdims=True)
        tail = jnp.where(lane == k, column, tail)
    o_ref[0, :rows, width:] = tail.astype(BF16)
    copies[1].wait()
    copies[2].wait()


def pack(x, g, ids):
    rows, width = x.shape
    return pl.pallas_call(
        pack_kernel,
        out_shape=pltpu.VMEM((1, 2 * rows, width + LANES), BF16),
        in_specs=[HBM] * 3,
        out_specs=VMEM,
        scratch_shapes=[pltpu.VMEM(ids.shape, jnp.int32), pltpu.SemaphoreType.DMA((3,))],
        name="pack",
        compiler_params=pltpu.CompilerParams(vmem_limit_bytes=1 << 20),
        cost_estimate=pl.CostEstimate(flops=0, bytes_accessed=8 * rows * width, transcendentals=0),
    )(*[pltpu.with_memory_space_constraint(a, pltpu.HBM) for a in (x, g, ids)])


def fetch_kernel(*refs):
    count = (len(refs) - 3) // 2
    sources, targets, sems = refs[:count], refs[count + 2 : -1], refs[-1]
    copies = [pltpu.make_async_copy(a, b, sems.at[i]) for i, (a, b) in enumerate(zip(sources, targets))]
    for copy in copies:
        copy.start()
    for copy in copies:
        copy.wait()


def fetch(after, me, *arrays):
    count = len(arrays)
    held = sum(a.size * a.dtype.itemsize for a in arrays)
    return pl.pallas_call(
        fetch_kernel,
        out_shape=[pltpu.VMEM(a.shape, a.dtype) for a in arrays],
        in_specs=[HBM] * count + [pl.BlockSpec(memory_space=pl.ANY), SMEM],
        out_specs=[VMEM] * count,
        scratch_shapes=[pltpu.SemaphoreType.DMA((count,))],
        name="fetch",
        compiler_params=pltpu.CompilerParams(vmem_limit_bytes=1 << 20),
        cost_estimate=pl.CostEstimate(flops=0, bytes_accessed=held, transcendentals=0),
    )(*[pltpu.with_memory_space_constraint(a, pltpu.HBM) for a in arrays], after, me)


def contract_last(left, right):
    return lax.dot_general(left, right, (((1,), (1,)), ((), ())), preferred_element_type=F32)


def thirds(value):
    high = value.astype(BF16)
    rest = value - high.astype(F32)
    middle = rest.astype(BF16)
    return high, middle, (rest - middle.astype(F32)).astype(BF16)


def expert_kernel(top, me_ref, gain_ref, router_ref, wg_ref, wu_ref, wd_hbm, *refs):
    pieces, outs = refs[:8], refs[8:16]
    nb, sg, gate_s, up_s, out_s, hid_s, dg_s, du_s, route_s, wd_ref, wd_sem = refs[16:]
    wd_copy = pltpu.make_async_copy(wd_hbm, wd_ref, wd_sem)
    wd_copy.start()
    blocks, double, _ = pieces[0].shape
    rows = double // 2
    width, units = wg_ref.shape
    step_f = units
    step_d = width
    mine = me_ref[0]
    gain = gain_ref[...]
    router = router_ref[...]
    r_hi, r_mid, r_lo = thirds(router)
    split = jnp.concatenate([r_hi, r_mid, r_lo], axis=0)
    route_s[...] = jnp.concatenate([r_hi, r_mid, r_lo, r_hi, r_mid, r_hi], axis=0)
    routes = route_s
    total_rows = 8 * rows
    lane = lax.broadcasted_iota(jnp.int32, (total_rows, EXPERTS), 1)

    def block(h, carry):
        x = jnp.concatenate([p[h, :rows, :width].astype(F32) for p in pieces], axis=0)
        dy = jnp.concatenate([p[h, rows:, :width].astype(F32) for p in pieces], axis=0)
        ids = jnp.concatenate([p[h, :rows, width:].astype(F32) for p in pieces], axis=0)
        inv = lax.rsqrt(jnp.mean(x * x, axis=-1, keepdims=True) + EPS)
        nb[...] = (x * inv * gain).astype(BF16)
        parts = contract_last(nb[...], split)
        logits = parts[:, :EXPERTS] + parts[:, EXPERTS : 2 * EXPERTS] + parts[:, 2 * EXPERTS :]
        affinity = 1.0 / (1.0 + jnp.exp(-logits))
        chosen = jnp.zeros((total_rows, EXPERTS), F32)
        for k in range(top):
            chosen += (ids[:, k : k + 1].astype(jnp.int32) == lane).astype(F32)
        total = jnp.sum(chosen * affinity, axis=-1, keepdims=True)
        here = chosen * (lane == mine).astype(F32)
        has = jnp.sum(here, axis=-1, keepdims=True)
        weight = jnp.sum(here * affinity, axis=-1, keepdims=True) / total
        sg[...] = (weight * dy).astype(BF16)

        def first(n, c):
            cols = pl.ds(n * step_f, step_f)
            gate_s[:, cols] = jnp.dot(nb[...], wg_ref[:, cols], preferred_element_type=F32)
            up_s[:, cols] = jnp.dot(nb[...], wu_ref[:, cols], preferred_element_type=F32)
            return c

        for n in range(units // step_f):
            first(n, 0)
        gate = gate_s[...]
        up = up_s[...]
        sigma = 1.0 / (1.0 + jnp.exp(-gate))
        active = gate * sigma
        slope = sigma * (1.0 + gate * (1.0 - sigma))
        hid_s[...] = (active * up).astype(BF16)

        if blocks == 1:
            wd_copy.wait()

        def second(n, c):
            cols = pl.ds(n * step_d, step_d)
            out_s[:, cols] = jnp.dot(hid_s[...], wd_ref[:, cols], preferred_element_type=F32)
            return c

        for n in range(width // step_d):
            second(n, 0)
        out = out_s[...]
        dweight = has * jnp.sum(dy * out, axis=-1, keepdims=True)
        share = (weight * out).astype(BF16)
        for q in range(8):
            outs[q][h, :rows, :] = share[q * rows : (q + 1) * rows]
        coef = chosen * affinity * (1.0 - affinity) * ((lane == mine).astype(F32) - weight)
        coef = coef * (dweight / total)
        c_hi, c_mid, c_lo = thirds(coef)
        coefs = jnp.concatenate([c_hi, c_hi, c_hi, c_mid, c_mid, c_lo], axis=1)

        def third(n, c):
            cols = pl.ds(n * step_f, step_f)
            gate_s[:, cols] = contract_last(sg[...], wd_ref[cols, :])
            return c

        for n in range(units // step_f):
            third(n, 0)
        dhidden = gate_s[...]
        dg_s[...] = (dhidden * up * slope).astype(BF16)
        du_s[...] = (dhidden * active).astype(BF16)

        def fourth(n, c):
            cols = pl.ds(n * step_d, step_d)
            out_s[:, cols] = (
                contract_last(dg_s[...], wg_ref[cols, :])
                + contract_last(du_s[...], wu_ref[cols, :])
                + jnp.dot(coefs, routes[:, cols], preferred_element_type=F32)
            )
            return c

        for n in range(width // step_d):
            fourth(n, 0)
        u = out_s[...] * gain
        x = jnp.concatenate([p[h, :rows, :width].astype(F32) for p in pieces], axis=0)
        m = jnp.mean(u * x, axis=-1, keepdims=True)
        din = (inv * u - x * (inv * inv * inv * m)).astype(BF16)
        for q in range(8):
            outs[q][h, rows:, :] = din[q * rows : (q + 1) * rows]
        return carry

    if blocks == 1:
        block(0, 0)
    else:
        wd_copy.wait()
        lax.fori_loop(0, blocks, block, 0)


def experts(top, me, gain, router, wg, wu, wd, pieces):
    blocks, double, _ = pieces[0].shape
    width, units = wg.shape
    total = 8 * double // 2
    return pl.pallas_call(
        functools.partial(expert_kernel, top),
        out_shape=[jax.ShapeDtypeStruct((blocks, double, width), BF16)] * 8,
        in_specs=[SMEM] + [VMEM] * 4 + [HBM] + [VMEM] * 8,
        out_specs=[VMEM] * 8,
        scratch_shapes=[
            pltpu.VMEM((total, width), BF16),
            pltpu.VMEM((total, width), BF16),
            pltpu.VMEM((total, units), F32),
            pltpu.VMEM((total, units), F32),
            pltpu.VMEM((total, width), F32),
            pltpu.VMEM((total, units), BF16),
            pltpu.VMEM((total, units), BF16),
            pltpu.VMEM((total, units), BF16),
            pltpu.VMEM((6 * EXPERTS, width), BF16),
            pltpu.VMEM((units, width), BF16),
            pltpu.SemaphoreType.DMA,
        ],
        compiler_params=pltpu.CompilerParams(vmem_limit_bytes=VMEM_LIMIT),
        name="experts",
    )(me, gain, router, wg, wu, wd, *pieces)


VMEM_LIMIT = 24 << 20


def add(a, b):
    return (a.astype(F32) + b.astype(F32)).astype(BF16)


def section_step(acts, grads, norm_gain, router, w_gate, w_up, w_down, expert_ids):
    x, dy, ids = acts[0], grads[0], expert_ids[0]
    rows, _ = x.shape
    count = lax.axis_size("expert")
    groups = count // EXPERTS
    me = (lax.axis_index("expert") // groups).astype(jnp.int32).reshape(1)
    own = pack(x, dy, ids.T)
    bit = 8
    while bit < count:
        own = jnp.concatenate([own, flip(own, bit)], axis=0)
        bit *= 2
    wg, wu, route, gain = fetch(own, me, w_gate[0], w_up[0], router[0].T, norm_gain)
    pieces = {0: own}
    for j in (6, 2, 4):
        pieces[j] = flip(own, j)
    for j in (0, 2, 4, 6):
        pieces[j + 1] = flip(pieces[j], 1)
    outs = experts(
        ids.shape[1], me, gain, route, wg, wu, pltpu.with_memory_space_constraint(w_down[0], pltpu.HBM),
        [pieces[j] for j in range(8)],
    )
    kept = {j: add(outs[j], flip(outs[j + 1], 1)) for j in (6, 2, 4, 0)}
    came = [flip(kept[j], j) for j in (6, 2, 4)]
    if count > 8:
        got = kept[0].astype(F32) + sum(c.astype(F32) for c in came)
        bit = count // 2
        while bit >= 8:
            half = got.shape[0] // 2
            got = got[:half] + flip(got[half:].astype(BF16), bit).astype(F32)
            bit //= 2
    else:
        got = kept[0].astype(F32) + sum(c.astype(F32) for c in came)
    section_out = (x.astype(F32) + got[0, :rows]).astype(BF16)
    section_grad = (dy.astype(F32) + got[0, rows:]).astype(BF16)
    stages = lax.axis_size("pipe")
    odd = lax.axis_index("pipe") % 2 == 1
    first = jnp.where(odd, section_grad, section_out)
    second = jnp.where(odd, section_out, section_grad)

    def trade(value, parity):
        pairs = []
        for s in range(parity, stages - 1, 2):
            pairs += [(s, s + 1), (s + 1, s)]
        return lax.ppermute(value, "pipe", pairs)

    first = trade(first, 0)
    second = trade(second, 1)
    arrived = jnp.where(odd, first, second)
    returned = jnp.where(odd, second, first)
    return (arrived[None], returned[None])


def solution(mesh):
    return jax.shard_map(
        section_step,
        mesh=mesh,
        in_specs=(
            P("pipe", "expert", None),
            P("pipe", "expert", None),
            P("pipe", None),
            P("pipe", None, None),
            P("pipe", None, "expert"),
            P("pipe", None, "expert"),
            P("pipe", "expert", None),
            P("pipe", "expert", None),
        ),
        out_specs=(P("pipe", "expert", None), P("pipe", "expert", None)),
        check_vma=False,
    )
```

```python
import functools
import jax
import jax.numpy as jnp
from jax import lax
from jax.experimental import pallas as pl
from jax.experimental.pallas import tpu as pltpu
from jax.sharding import PartitionSpec as P

EXPERTS = 8
LANES = 128
EPS = 1e-06
F32 = jnp.float32
BF16 = jnp.bfloat16


VMEM = pl.BlockSpec(memory_space=pltpu.VMEM)
HBM = pl.BlockSpec(memory_space=pltpu.HBM)
SMEM = pl.BlockSpec(memory_space=pltpu.SMEM)


def flip(value, bit):
    count = lax.axis_size("expert")
    return lax.ppermute(value, "expert", [(i, i ^ bit) for i in range(count)])


def pack_kernel(x_hbm, g_hbm, ids_hbm, o_ref, ids_ref, sems):
    rows, width = x_hbm.shape
    copies = [
        pltpu.make_async_copy(ids_hbm, ids_ref, sems.at[0]),
        pltpu.make_async_copy(x_hbm, o_ref.at[0, pl.ds(0, rows), pl.ds(0, width)], sems.at[1]),
        pltpu.make_async_copy(g_hbm, o_ref.at[0, pl.ds(rows, rows), pl.ds(0, width)], sems.at[2]),
    ]
    for copy in copies:
        copy.start()
    o_ref[0, rows:, width:] = jnp.zeros((rows, LANES), BF16)
    lane = lax.broadcasted_iota(jnp.int32, (rows, LANES), 1)
    across = lax.broadcasted_iota(jnp.int32, (rows, rows), 1)
    down = lax.broadcasted_iota(jnp.int32, (rows, rows), 0)
    copies[0].wait()
    ids = ids_ref[...].astype(F32)
    tail = jnp.zeros((rows, LANES), F32)
    for k in range(ids.shape[0]):
        column = jnp.sum(jnp.where(across == down, ids[k : k + 1, :], 0.0), axis=1, keepdims=True)
        tail = jnp.where(lane == k, column, tail)
    o_ref[0, :rows, width:] = tail.astype(BF16)
    copies[1].wait()
    copies[2].wait()


def pack(x, g, ids):
    rows, width = x.shape
    return pl.pallas_call(
        pack_kernel,
        out_shape=pltpu.VMEM((1, 2 * rows, width + LANES), BF16),
        in_specs=[HBM] * 3,
        out_specs=VMEM,
        scratch_shapes=[pltpu.VMEM(ids.shape, jnp.int32), pltpu.SemaphoreType.DMA((3,))],
        name="pack",
        compiler_params=pltpu.CompilerParams(vmem_limit_bytes=1 << 20),
        cost_estimate=pl.CostEstimate(flops=0, bytes_accessed=8 * rows * width, transcendentals=0),
    )(*[pltpu.with_memory_space_constraint(a, pltpu.HBM) for a in (x, g, ids)])


def fetch_kernel(*refs):
    count = (len(refs) - 3) // 2
    sources, targets, sems = refs[:count], refs[count + 2 : -1], refs[-1]
    copies = [pltpu.make_async_copy(a, b, sems.at[i]) for i, (a, b) in enumerate(zip(sources, targets))]
    for copy in copies:
        copy.start()
    for copy in copies:
        copy.wait()


def fetch(after, me, *arrays):
    count = len(arrays)
    held = sum(a.size * a.dtype.itemsize for a in arrays)
    return pl.pallas_call(
        fetch_kernel,
        out_shape=[pltpu.VMEM(a.shape, a.dtype) for a in arrays],
        in_specs=[HBM] * count + [pl.BlockSpec(memory_space=pl.ANY), SMEM],
        out_specs=[VMEM] * count,
        scratch_shapes=[pltpu.SemaphoreType.DMA((count,))],
        name="fetch",
        compiler_params=pltpu.CompilerParams(vmem_limit_bytes=1 << 20),
        cost_estimate=pl.CostEstimate(flops=0, bytes_accessed=held, transcendentals=0),
    )(*[pltpu.with_memory_space_constraint(a, pltpu.HBM) for a in arrays], after, me)


def contract_last(left, right):
    return lax.dot_general(left, right, (((1,), (1,)), ((), ())), preferred_element_type=F32)


def thirds(value):
    high = value.astype(BF16)
    rest = value - high.astype(F32)
    middle = rest.astype(BF16)
    return high, middle, (rest - middle.astype(F32)).astype(BF16)


def expert_kernel(top, me_ref, gain_ref, router_ref, wg_ref, wu_ref, wd_hbm, *refs):
    pieces, evens, last, rest = refs[:8], refs[8:12], refs[12], refs[13]
    outs = [evens[q // 2] if q % 2 == 0 else last if q == 7 else rest.at[q // 2] for q in range(8)]
    nb, sg, gate_s, up_s, out_s, hid_s, dg_s, du_s, route_s, wd_ref, wd_sem = refs[14:]
    wd_copy = pltpu.make_async_copy(wd_hbm, wd_ref, wd_sem)
    wd_copy.start()
    blocks, double, _ = pieces[0].shape
    rows = double // 2
    width, units = wg_ref.shape
    step_f = units
    step_d = width
    mine = me_ref[0]
    gain = gain_ref[...]
    router = router_ref[...]
    r_hi, r_mid, r_lo = thirds(router)
    split = jnp.concatenate([r_hi, r_mid, r_lo], axis=0)
    route_s[...] = jnp.concatenate([r_hi, r_mid, r_lo, r_hi, r_mid, r_hi], axis=0)
    routes = route_s
    total_rows = 8 * rows
    lane = lax.broadcasted_iota(jnp.int32, (total_rows, EXPERTS), 1)

    def block(h, carry):
        x = jnp.concatenate([p[h, :rows, :width].astype(F32) for p in pieces], axis=0)
        dy = jnp.concatenate([p[h, rows:, :width].astype(F32) for p in pieces], axis=0)
        ids = jnp.concatenate([p[h, :rows, width:].astype(F32) for p in pieces], axis=0)
        inv = lax.rsqrt(jnp.mean(x * x, axis=-1, keepdims=True) + EPS)
        nb[...] = (x * inv * gain).astype(BF16)
        parts = contract_last(nb[...], split)
        logits = parts[:, :EXPERTS] + parts[:, EXPERTS : 2 * EXPERTS] + parts[:, 2 * EXPERTS :]
        affinity = 1.0 / (1.0 + jnp.exp(-logits))
        chosen = jnp.zeros((total_rows, EXPERTS), F32)
        for k in range(top):
            chosen += (ids[:, k : k + 1].astype(jnp.int32) == lane).astype(F32)
        total = jnp.sum(chosen * affinity, axis=-1, keepdims=True)
        here = chosen * (lane == mine).astype(F32)
        has = jnp.sum(here, axis=-1, keepdims=True)
        weight = jnp.sum(here * affinity, axis=-1, keepdims=True) / total
        sg[...] = (weight * dy).astype(BF16)

        def first(n, c):
            cols = pl.ds(n * step_f, step_f)
            gate_s[:, cols] = jnp.dot(nb[...], wg_ref[:, cols], preferred_element_type=F32)
            up_s[:, cols] = jnp.dot(nb[...], wu_ref[:, cols], preferred_element_type=F32)
            return c

        for n in range(units // step_f):
            first(n, 0)
        gate = gate_s[...]
        up = up_s[...]
        sigma = 1.0 / (1.0 + jnp.exp(-gate))
        active = gate * sigma
        slope = sigma * (1.0 + gate * (1.0 - sigma))
        hid_s[...] = (active * up).astype(BF16)

        if blocks == 1:
            wd_copy.wait()

        def second(n, c):
            cols = pl.ds(n * step_d, step_d)
            out_s[:, cols] = jnp.dot(hid_s[...], wd_ref[:, cols], preferred_element_type=F32)
            return c

        for n in range(width // step_d):
            second(n, 0)
        out = out_s[...]
        dweight = has * jnp.sum(dy * out, axis=-1, keepdims=True)
        share = (weight * out).astype(BF16)
        for q in range(8):
            outs[q][h, :rows, :] = share[q * rows : (q + 1) * rows]
        coef = chosen * affinity * (1.0 - affinity) * ((lane == mine).astype(F32) - weight)
        coef = coef * (dweight / total)
        c_hi, c_mid, c_lo = thirds(coef)
        coefs = jnp.concatenate([c_hi, c_hi, c_hi, c_mid, c_mid, c_lo], axis=1)

        def third(n, c):
            cols = pl.ds(n * step_f, step_f)
            gate_s[:, cols] = contract_last(sg[...], wd_ref[cols, :])
            return c

        for n in range(units // step_f):
            third(n, 0)
        dhidden = gate_s[...]
        dg_s[...] = (dhidden * up * slope).astype(BF16)
        du_s[...] = (dhidden * active).astype(BF16)

        def fourth(n, c):
            cols = pl.ds(n * step_d, step_d)
            out_s[:, cols] = (
                contract_last(dg_s[...], wg_ref[cols, :])
                + contract_last(du_s[...], wu_ref[cols, :])
                + jnp.dot(coefs, routes[:, cols], preferred_element_type=F32)
            )
            return c

        for n in range(width // step_d):
            fourth(n, 0)
        u = out_s[...] * gain
        x = jnp.concatenate([p[h, :rows, :width].astype(F32) for p in pieces], axis=0)
        m = jnp.mean(u * x, axis=-1, keepdims=True)
        din = (inv * u - x * (inv * inv * inv * m)).astype(BF16)
        for q in range(8):
            outs[q][h, rows:, :] = din[q * rows : (q + 1) * rows]
        return carry

    if blocks == 1:
        block(0, 0)
    else:
        wd_copy.wait()
        lax.fori_loop(0, blocks, block, 0)


def experts(top, me, gain, router, wg, wu, wd, pieces):
    blocks, double, _ = pieces[0].shape
    width, units = wg.shape
    total = 8 * double // 2
    return pl.pallas_call(
        functools.partial(expert_kernel, top),
        out_shape=[jax.ShapeDtypeStruct((blocks, double, width), BF16)] * 5
        + [jax.ShapeDtypeStruct((3, blocks, double, width), BF16)],
        in_specs=[SMEM] + [VMEM] * 4 + [HBM] + [VMEM] * 8,
        out_specs=[VMEM] * 6,
        scratch_shapes=[
            pltpu.VMEM((total, width), BF16),
            pltpu.VMEM((total, width), BF16),
            pltpu.VMEM((total, units), F32),
            pltpu.VMEM((total, units), F32),
            pltpu.VMEM((total, width), F32),
            pltpu.VMEM((total, units), BF16),
            pltpu.VMEM((total, units), BF16),
            pltpu.VMEM((total, units), BF16),
            pltpu.VMEM((6 * EXPERTS, width), BF16),
            pltpu.VMEM((units, width), BF16),
            pltpu.SemaphoreType.DMA,
        ],
        compiler_params=pltpu.CompilerParams(vmem_limit_bytes=VMEM_LIMIT),
        name="experts",
    )(me, gain, router, wg, wu, wd, *pieces)


VMEM_LIMIT = 24 << 20


def add(a, b):
    return (a.astype(F32) + b.astype(F32)).astype(BF16)


def section_step(acts, grads, norm_gain, router, w_gate, w_up, w_down, expert_ids):
    x, dy, ids = acts[0], grads[0], expert_ids[0]
    rows, _ = x.shape
    count = lax.axis_size("expert")
    groups = count // EXPERTS
    me = (lax.axis_index("expert") // groups).astype(jnp.int32).reshape(1)
    own = pack(x, dy, ids.T)
    bit = 8
    while bit < count:
        own = jnp.concatenate([own, flip(own, bit)], axis=0)
        bit *= 2
    wg, wu, route, gain = fetch(own, me, w_gate[0], w_up[0], router[0].T, norm_gain)
    pieces = {0: own}
    for j in (6, 2, 4):
        pieces[j] = flip(own, j)
    for j in (0, 2, 4, 6):
        pieces[j + 1] = flip(pieces[j], 1)
    outs = experts(
        ids.shape[1], me, gain, route, wg, wu, pltpu.with_memory_space_constraint(w_down[0], pltpu.HBM),
        [pieces[j] for j in range(8)],
    )
    evens, last, rest = outs[:4], outs[4], outs[5]
    kept = {6: add(evens[3], flip(last, 1))}
    rest = flip(rest, 1)
    for j in (2, 4, 0):
        kept[j] = add(evens[j // 2], rest[j // 2])
    came = [flip(kept[j], j) for j in (6, 2, 4)]
    if count > 8:
        got = kept[0].astype(F32) + sum(c.astype(F32) for c in came)
        bit = count // 2
        while bit >= 8:
            half = got.shape[0] // 2
            got = got[:half] + flip(got[half:].astype(BF16), bit).astype(F32)
            bit //= 2
    else:
        got = kept[0].astype(F32) + sum(c.astype(F32) for c in came)
    section_out = (x.astype(F32) + got[0, :rows]).astype(BF16)
    section_grad = (dy.astype(F32) + got[0, rows:]).astype(BF16)
    stages = lax.axis_size("pipe")
    odd = lax.axis_index("pipe") % 2 == 1
    first = jnp.where(odd, section_grad, section_out)
    second = jnp.where(odd, section_out, section_grad)

    def trade(value, parity):
        pairs = []
        for s in range(parity, stages - 1, 2):
            pairs += [(s, s + 1), (s + 1, s)]
        return lax.ppermute(value, "pipe", pairs)

    first = trade(first, 0)
    second = trade(second, 1)
    arrived = jnp.where(odd, first, second)
    returned = jnp.where(odd, second, first)
    return (arrived[None], returned[None])


def solution(mesh):
    return jax.shard_map(
        section_step,
        mesh=mesh,
        in_specs=(
            P("pipe", "expert", None),
            P("pipe", "expert", None),
            P("pipe", None),
            P("pipe", None, None),
            P("pipe", None, "expert"),
            P("pipe", None, "expert"),
            P("pipe", "expert", None),
            P("pipe", "expert", None),
        ),
        out_specs=(P("pipe", "expert", None), P("pipe", "expert", None)),
        check_vma=False,
    )
```

```python
import functools
import jax
import jax.numpy as jnp
from jax import lax
from jax.experimental import pallas as pl
from jax.experimental.pallas import tpu as pltpu
from jax.sharding import PartitionSpec as P

EXPERTS = 8
LANES = 128
EPS = 1e-06
F32 = jnp.float32
BF16 = jnp.bfloat16


VMEM = pl.BlockSpec(memory_space=pltpu.VMEM)
HBM = pl.BlockSpec(memory_space=pltpu.HBM)
SMEM = pl.BlockSpec(memory_space=pltpu.SMEM)


def flip(value, bit):
    count = lax.axis_size("expert")
    return lax.ppermute(value, "expert", [(i, i ^ bit) for i in range(count)])


def pack_kernel(x_hbm, g_hbm, ids_hbm, o_ref, ids_ref, sems):
    rows, width = x_hbm.shape
    copies = [
        pltpu.make_async_copy(ids_hbm, ids_ref, sems.at[0]),
        pltpu.make_async_copy(x_hbm, o_ref.at[0, pl.ds(0, rows), pl.ds(0, width)], sems.at[1]),
        pltpu.make_async_copy(g_hbm, o_ref.at[0, pl.ds(rows, rows), pl.ds(0, width)], sems.at[2]),
    ]
    for copy in copies:
        copy.start()
    o_ref[0, rows:, width:] = jnp.zeros((rows, LANES), BF16)
    lane = lax.broadcasted_iota(jnp.int32, (rows, LANES), 1)
    across = lax.broadcasted_iota(jnp.int32, (rows, rows), 1)
    down = lax.broadcasted_iota(jnp.int32, (rows, rows), 0)
    copies[0].wait()
    ids = ids_ref[...].astype(F32)
    tail = jnp.zeros((rows, LANES), F32)
    for k in range(ids.shape[0]):
        column = jnp.sum(jnp.where(across == down, ids[k : k + 1, :], 0.0), axis=1, keepdims=True)
        tail = jnp.where(lane == k, column, tail)
    o_ref[0, :rows, width:] = tail.astype(BF16)
    copies[1].wait()
    copies[2].wait()


def pack(x, g, ids):
    rows, width = x.shape
    return pl.pallas_call(
        pack_kernel,
        out_shape=pltpu.VMEM((1, 2 * rows, width + LANES), BF16),
        in_specs=[HBM] * 3,
        out_specs=VMEM,
        scratch_shapes=[pltpu.VMEM(ids.shape, jnp.int32), pltpu.SemaphoreType.DMA((3,))],
        name="pack",
        compiler_params=pltpu.CompilerParams(vmem_limit_bytes=1 << 20),
        cost_estimate=pl.CostEstimate(flops=0, bytes_accessed=8 * rows * width, transcendentals=0),
    )(*[pltpu.with_memory_space_constraint(a, pltpu.HBM) for a in (x, g, ids)])


def fetch_kernel(*refs):
    count = (len(refs) - 3) // 2
    sources, targets, sems = refs[:count], refs[count + 2 : -1], refs[-1]
    copies = [pltpu.make_async_copy(a, b, sems.at[i]) for i, (a, b) in enumerate(zip(sources, targets))]
    for copy in copies:
        copy.start()
    for copy in copies:
        copy.wait()


def fetch(after, me, *arrays):
    count = len(arrays)
    held = sum(a.size * a.dtype.itemsize for a in arrays)
    return pl.pallas_call(
        fetch_kernel,
        out_shape=[pltpu.VMEM(a.shape, a.dtype) for a in arrays],
        in_specs=[HBM] * count + [pl.BlockSpec(memory_space=pl.ANY), SMEM],
        out_specs=[VMEM] * count,
        scratch_shapes=[pltpu.SemaphoreType.DMA((count,))],
        name="fetch",
        compiler_params=pltpu.CompilerParams(vmem_limit_bytes=1 << 20),
        cost_estimate=pl.CostEstimate(flops=0, bytes_accessed=held, transcendentals=0),
    )(*[pltpu.with_memory_space_constraint(a, pltpu.HBM) for a in arrays], after, me)


def contract_last(left, right):
    return lax.dot_general(left, right, (((1,), (1,)), ((), ())), preferred_element_type=F32)


def thirds(value):
    high = value.astype(BF16)
    rest = value - high.astype(F32)
    middle = rest.astype(BF16)
    return high, middle, (rest - middle.astype(F32)).astype(BF16)


def expert_kernel(top, me_ref, gain_ref, router_ref, wg_ref, wu_ref, wd_hbm, *refs):
    pieces, evens, last, rest = refs[:8], refs[8:12], refs[12], refs[13]
    outs = [evens[q // 2] if q % 2 == 0 else last if q == 7 else rest.at[q // 2] for q in range(8)]
    nb, sg, gate_s, up_s, out_s, hid_s, dg_s, du_s, route_s, wd_ref, wd_sem = refs[14:]
    wd_copy = pltpu.make_async_copy(wd_hbm, wd_ref, wd_sem)
    wd_copy.start()
    blocks, double, _ = pieces[0].shape
    rows = double // 2
    width, units = wg_ref.shape
    step_f = units
    step_d = width
    mine = me_ref[0]
    gain = gain_ref[...]
    router = router_ref[...]
    r_hi, r_mid, r_lo = thirds(router)
    split = jnp.concatenate([r_hi, r_mid, r_lo], axis=0)
    route_s[...] = jnp.concatenate([r_hi, r_mid, r_lo, r_hi, r_mid, r_hi], axis=0)
    routes = route_s
    total_rows = 8 * rows
    lane = lax.broadcasted_iota(jnp.int32, (total_rows, EXPERTS), 1)

    def block(h, carry):
        x = jnp.concatenate([p[h, :rows, :width].astype(F32) for p in pieces], axis=0)
        dy = jnp.concatenate([p[h, rows:, :width].astype(F32) for p in pieces], axis=0)
        ids = jnp.concatenate([p[h, :rows, width:].astype(F32) for p in pieces], axis=0)
        inv = lax.rsqrt(jnp.mean(x * x, axis=-1, keepdims=True) + EPS)
        nb[...] = (x * inv * gain).astype(BF16)
        parts = contract_last(nb[...], split)
        logits = parts[:, :EXPERTS] + parts[:, EXPERTS : 2 * EXPERTS] + parts[:, 2 * EXPERTS :]
        affinity = 1.0 / (1.0 + jnp.exp(-logits))
        chosen = jnp.zeros((total_rows, EXPERTS), F32)
        for k in range(top):
            chosen += (ids[:, k : k + 1].astype(jnp.int32) == lane).astype(F32)
        total = jnp.sum(chosen * affinity, axis=-1, keepdims=True)
        here = chosen * (lane == mine).astype(F32)
        has = jnp.sum(here, axis=-1, keepdims=True)
        weight = jnp.sum(here * affinity, axis=-1, keepdims=True) / total
        sg[...] = (weight * dy).astype(BF16)

        def first(n, c):
            cols = pl.ds(n * step_f, step_f)
            gate_s[:, cols] = jnp.dot(nb[...], wg_ref[:, cols], preferred_element_type=F32)
            up_s[:, cols] = jnp.dot(nb[...], wu_ref[:, cols], preferred_element_type=F32)
            return c

        for n in range(units // step_f):
            first(n, 0)
        gate = gate_s[...]
        up = up_s[...]
        sigma = 1.0 / (1.0 + jnp.exp(-gate))
        active = gate * sigma
        slope = sigma * (1.0 + gate * (1.0 - sigma))
        hid_s[...] = (active * up).astype(BF16)

        if blocks == 1:
            wd_copy.wait()

        def second(n, c):
            cols = pl.ds(n * step_d, step_d)
            out_s[:, cols] = jnp.dot(hid_s[...], wd_ref[:, cols], preferred_element_type=F32)
            return c

        for n in range(width // step_d):
            second(n, 0)
        out = out_s[...]
        dweight = has * jnp.sum(dy * out, axis=-1, keepdims=True)
        share = (weight * out).astype(BF16)
        for q in range(8):
            outs[q][h, :rows, :] = share[q * rows : (q + 1) * rows]
        coef = chosen * affinity * (1.0 - affinity) * ((lane == mine).astype(F32) - weight)
        coef = coef * (dweight / total)
        c_hi, c_mid, c_lo = thirds(coef)
        coefs = jnp.concatenate([c_hi, c_hi, c_hi, c_mid, c_mid, c_lo], axis=1)

        def third(n, c):
            cols = pl.ds(n * step_f, step_f)
            gate_s[:, cols] = contract_last(sg[...], wd_ref[cols, :])
            return c

        for n in range(units // step_f):
            third(n, 0)
        dhidden = gate_s[...]
        dg_s[...] = (dhidden * up * slope).astype(BF16)
        du_s[...] = (dhidden * active).astype(BF16)

        def fourth(n, c):
            cols = pl.ds(n * step_d, step_d)
            out_s[:, cols] = (
                contract_last(dg_s[...], wg_ref[cols, :])
                + contract_last(du_s[...], wu_ref[cols, :])
                + jnp.dot(coefs, routes[:, cols], preferred_element_type=F32)
            )
            return c

        for n in range(width // step_d):
            fourth(n, 0)
        u = out_s[...] * gain
        x = jnp.concatenate([p[h, :rows, :width].astype(F32) for p in pieces], axis=0)
        m = jnp.mean(u * x, axis=-1, keepdims=True)
        din = (inv * u - x * (inv * inv * inv * m)).astype(BF16)
        for q in range(8):
            outs[q][h, rows:, :] = din[q * rows : (q + 1) * rows]
        return carry

    if blocks == 1:
        block(0, 0)
    else:
        wd_copy.wait()
        lax.fori_loop(0, blocks, block, 0)


def experts(top, me, gain, router, wg, wu, wd, pieces):
    blocks, double, _ = pieces[0].shape
    width, units = wg.shape
    total = 8 * double // 2
    return pl.pallas_call(
        functools.partial(expert_kernel, top),
        out_shape=[jax.ShapeDtypeStruct((blocks, double, width), BF16)] * 5
        + [jax.ShapeDtypeStruct((3, blocks, double, width), BF16)],
        in_specs=[SMEM] + [VMEM] * 4 + [HBM] + [VMEM] * 8,
        out_specs=[VMEM] * 6,
        scratch_shapes=[
            pltpu.VMEM((total, width), BF16),
            pltpu.VMEM((total, width), BF16),
            pltpu.VMEM((total, units), F32),
            pltpu.VMEM((total, units), F32),
            pltpu.VMEM((total, width), F32),
            pltpu.VMEM((total, units), BF16),
            pltpu.VMEM((total, units), BF16),
            pltpu.VMEM((total, units), BF16),
            pltpu.VMEM((6 * EXPERTS, width), BF16),
            pltpu.VMEM((units, width), BF16),
            pltpu.SemaphoreType.DMA,
        ],
        compiler_params=pltpu.CompilerParams(vmem_limit_bytes=VMEM_LIMIT),
        name="experts",
    )(me, gain, router, wg, wu, wd, *pieces)


VMEM_LIMIT = 24 << 20


def add(a, b):
    return (a.astype(F32) + b.astype(F32)).astype(BF16)


def section_step(acts, grads, norm_gain, router, w_gate, w_up, w_down, expert_ids):
    x, dy, ids = acts[0], grads[0], expert_ids[0]
    rows, _ = x.shape
    count = lax.axis_size("expert")
    groups = count // EXPERTS
    index = lax.axis_index("expert")
    stage = lax.axis_index("pipe")
    me = jnp.stack([index // groups, index, stage]).astype(jnp.int32)
    own = pack(x, dy, ids.T)
    bit = 8
    while bit < count:
        own = jnp.concatenate([own, flip(own, bit)], axis=0)
        bit *= 2
    wg, wu, route, gain = fetch(own, me, w_gate[0], w_up[0], router[0].T, norm_gain)
    pieces = {0: own}
    for j in (6, 2, 4):
        pieces[j] = flip(own, j)
    for j in (0, 2, 4, 6):
        pieces[j + 1] = flip(pieces[j], 1)
    outs = experts(
        ids.shape[1], me, gain, route, wg, wu, pltpu.with_memory_space_constraint(w_down[0], pltpu.HBM),
        [pieces[j] for j in range(8)],
    )
    outs, index, stage = lax.optimization_barrier((outs, index, stage))
    evens, last, rest = outs[:4], outs[4], outs[5]
    kept = {6: add(evens[3], flip(last, 1))}
    rest = flip(rest, 1)
    for j in (2, 4, 0):
        kept[j] = add(evens[j // 2], rest[j // 2])
    came = [flip(kept[j], j) for j in (6, 2, 4)]
    if count > 8:
        got = kept[0].astype(F32) + sum(c.astype(F32) for c in came)
        bit = count // 2
        while bit >= 8:
            half = got.shape[0] // 2
            got = got[:half] + flip(got[half:].astype(BF16), bit).astype(F32)
            bit //= 2
    else:
        got = kept[0].astype(F32) + sum(c.astype(F32) for c in came)
    section_out = (x.astype(F32) + got[0, :rows]).astype(BF16)
    section_grad = (dy.astype(F32) + got[0, rows:]).astype(BF16)
    stages = lax.axis_size("pipe")
    odd = lax.rem(stage + index, 2) == 1
    first = jnp.where(odd, section_grad, section_out)
    second = jnp.where(odd, section_out, section_grad)

    def trade(value, parity):
        pairs = []
        for s in range(stages - 1):
            for i in range((s + parity) % 2, count, 2):
                low, high = s * count + i, (s + 1) * count + i
                pairs += [(low, high), (high, low)]
        return lax.ppermute(value, ("pipe", "expert"), pairs)

    first = trade(first, 0)
    second = trade(second, 1)
    arrived = jnp.where(odd, first, second)
    returned = jnp.where(odd, second, first)
    return (arrived[None], returned[None])


def solution(mesh):
    return jax.shard_map(
        section_step,
        mesh=mesh,
        in_specs=(
            P("pipe", "expert", None),
            P("pipe", "expert", None),
            P("pipe", None),
            P("pipe", None, None),
            P("pipe", None, "expert"),
            P("pipe", None, "expert"),
            P("pipe", "expert", None),
            P("pipe", "expert", None),
        ),
        out_specs=(P("pipe", "expert", None), P("pipe", "expert", None)),
        check_vma=False,
    )
```
